32 devices in a mesh: region: 4 (over y, x), wave: 8 (over z, core).
Axes of the slice: x: 2, y: 2, z: 4, core: 2. Of those that a mesh axis runs over, the one named last changes fastest.
Arguments:
- state0: float32 [9, 35, 8192], P(None, None, ('region', 'wave')), may hold values from -6 to 6
- delta: float32 [9, 35, 8192], P(None, None, ('region', 'wave')), may hold values from -6 to 6
- adjoint: float32 [9, 35, 8192], P(None, None, ('region', 'wave')), may hold values from -6 to 6
- model: float32 [3, 35, 8192], P(None, None, ('region', 'wave')), may hold values from 0.5 to 2
- geometry: float32 [9, 8192], P(None, ('region', 'wave')), may hold values from -4 to 4
- normals: float32 [3, 4, 8192], P(None, None, ('region', 'wave')), may hold values from -1 to 1
- face_scale: float32 [4, 8192], P(None, ('region', 'wave')), may hold values from 0.5 to 2
- derivative: float32 [3, 35, 35], replicated, may hold values from -1 to 1
- lift: float32 [4, 35, 15], replicated, may hold values from -1.5 to 1.5
- prolong: float32 [8, 35, 10], replicated, may hold values from -2 to 2
- coarse_step: float32 [30, 1024], P(None, ('region', 'wave')), may hold values from -6 to 6
- reg_weight: float32 [30, 1024], P(None, ('region', 'wave')), may hold values from 1 to 10
- observe: float32 [35, 8192], P(None, ('region', 'wave')), may hold values from 0.1 to 1
- owner: int32 [8192, 1], P(('region', 'wave')), may hold values from 0 to 31; in each aligned block of 256 rows (0 to 255, 256 to 511, ...) at most 16 rows name the same one
- coarse_local: int32 [8192], P(('region', 'wave')), may hold values from 0 to 31
- child: int32 [8192], P(('region', 'wave')), may hold values from 0 to 7
- neighbor: int32 [4, 8192], P(None, ('region', 'wave')), may hold values from 0 to 1151
- orient: int32 [4, 8192], P(None, ('region', 'wave')), may hold values from 0 to 5
- send_face: int32 [4096], P(('region', 'wave')), may hold values from 0 to 1023
Outputs:
- delta_next: float32 [9, 35, 8192], P(None, None, ('region', 'wave'))
- adjoint_next: float32 [9, 35, 8192], P(None, None, ('region', 'wave'))
- hess_vec: float32 [30, 1024], P(None, ('region', 'wave'))
The draws below stay inside these ranges and needn't reach their ends.
Inputs may be any that keep to these rules, and one draw needn't show every extreme that they name: `owner`: no more than 16 fine elements of one device have coarse elements owned by one device, and that number is reached. `send_face`: entries w * 16 to w * 16 + 15 of a device name its traces for wave partition w.
All inputs are finite; a program needn't handle non-finite values.
Results may differ from the reference program's by a relative error of at most 0.0003.
Values sent between devices are 32-bit elements; how exact they have to be, the bound alone decides.
No kernel may reach another device: no remote copies, remote signals or barrier semaphores. Data moves between devices by JAX's collectives and lax.ppermute only.
A program may use at most 128 MiB of HBM per device.

```python
import math
import jax
import jax.numpy as jnp
import numpy as np
from jax import lax

FIELDS = 9
NODES = 35
FACE_NODES = 15
PARAMS = 3
PMODES = 10
CHILDREN = 8
E_DEV = 256
CB_DEV = 32
CAP = 16
CAPF = 16
TABLE = 1152
BLOCK = 30
FINE = 8192
COARSE = 1024
SENT = 4096
N_REGION = 4
N_WAVE = 8
DEVICES = 32


def place_ends(values, key, low, largest):
    longest = values.shape.index(max(values.shape))
    spots = []
    for shift in (0, 1):
        where = [jax.random.randint(jax.random.fold_in(key, axis), (), 0, length) for axis, length in enumerate(values.shape)]
        where[longest] = (where[longest] + shift) % values.shape[longest]
        spots.append(tuple(where))
    return values.at[spots[0]].set(low).at[spots[1]].set(largest)


def levels(rng, extent, split, low, top_value):
    loudness, own = 1.0, jax.random.fold_in(rng, 6)
    for axis_at, blocks in split:
        steps = jnp.exp(jax.random.uniform(jax.random.fold_in(own, axis_at), (blocks,), jnp.float32, low / len(split), top_value / len(split)))
        loudness = loudness * jnp.repeat(steps, extent[axis_at] // blocks).reshape([-1 if axis == axis_at else 1 for axis in range(len(extent))])
    return loudness


def routed_block(stream_key, own, number, rows, number_of, top, most, slope):
    order = jax.random.permutation(stream_key, number_of)
    heavy_load, common = load_shares(number_of, rows * top, most, slope, True), load_shares(number_of, rows * top, most, slope, False)
    places = jnp.arange(number_of)

    def named(lengths, turn):
        used = int((lengths > 0).sum())
        fixed = max(1, used // 4)
        shifted = fixed + (places - fixed + turn * (used - fixed)) % max(1, number_of - fixed)
        return jnp.zeros((number_of,), jnp.int32).at[order[jnp.where(places < fixed, places, shifted)]].set(jnp.asarray(lengths, jnp.int32))

    lengths = jnp.where(number % 4 == 0, named(heavy_load, number // 4), named(common, number - number // 4 - 1))
    mixed = jax.random.permutation(jax.random.fold_in(own, 3), number_of)
    donor, sink = mixed[0:number_of // 2 * 2:2], mixed[1:number_of // 2 * 2:2]
    slack = jnp.minimum(lengths[donor] - 1, most - lengths[sink]) // 2
    slack = jnp.where((donor == order[0]) | (sink == order[0]) | (lengths[sink] == 0), 0, jnp.maximum(slack, 0))
    shifted = jax.random.randint(jax.random.fold_in(own, 4), (number_of // 2,), 0, 1 << 20) % (slack + 1)
    lengths = lengths.at[donor].add(-shifted).at[sink].add(shifted)
    labels = jnp.searchsorted(jnp.cumsum(lengths), jnp.arange(rows * top), side="right").astype(jnp.int32)
    table = labels.reshape(top, rows).T
    table = table[jax.random.permutation(jax.random.fold_in(own, 1), rows)]
    turn = jax.random.randint(jax.random.fold_in(own, 2), (rows, 1), 0, top)
    return jnp.take_along_axis(table, (jnp.arange(top)[None, :] + turn) % top, axis=1)


def load_shares(amount, total, bound, slope, full):
    loads = [(1 << 20) // math.isqrt(standing ** slope) + 1 for standing in range(1, amount + 1)]
    largest = bound if full else min(bound, max(-(-total // amount), total * loads[0] // sum(loads)))
    least = 1 if total - largest >= amount - 1 else 0
    given, surplus = [largest] + [least] * (amount - 1), total - largest - least * (amount - 1)
    while surplus > 0:
        free = [i for i in range(1, amount) if given[i] < largest] or [i for i in range(1, amount) if given[i] < bound]
        whole, budget = sum([loads[i] for i in free]), surplus
        for i in free:
            addition = min(bound - given[i], max(1, budget * loads[i] // whole), surplus)
            given[i] = given[i] + addition
            surplus = surplus - addition
    return np.array(given)


def noise(key, dims, spread, bound, split=(), kind=jnp.bfloat16):
    drawn = jax.random.normal(key, dims, jnp.float32) * spread
    if len(split) > 0:
        drawn = levels(key, dims, split, -0.22, 0.18) * drawn
    return jnp.clip(drawn, min=-bound, max=bound).astype(kind)


def setup_inputs(seed: int = 0) -> dict:
    splits = jax.random.split(jax.random.key(seed), 20)
    state0 = noise(splits[0], (FIELDS, NODES, FINE), 1.0, 6.0, ((2, 32),), jnp.float32)
    delta = noise(splits[1], (FIELDS, NODES, FINE), 1.0, 6.0, ((2, 32),), jnp.float32)
    adjoint = noise(splits[2], (FIELDS, NODES, FINE), 1.0, 6.0, ((2, 32),), jnp.float32)
    model = jnp.clip(jnp.exp(math.log(2.0) - 1.3862944 * jax.random.uniform(splits[3], (PARAMS, NODES, FINE), jnp.float32) ** levels(splits[3], (PARAMS, NODES, FINE), ((2, 32),), -0.2, 0.2)), 0.5, 2.0)
    geometry = noise(splits[4], (9, FINE), 0.6, 4.0, ((1, 32),), jnp.float32)
    normals = jnp.clip(jax.random.uniform(splits[5], (3, 4, FINE), jnp.float32, -1.0, 1.0) * levels(splits[5], (3, 4, FINE), ((2, 32),), -0.4, 0.0), -1.0, 1.0)
    face_scale = jnp.clip(jnp.exp(math.log(2.0) - 1.3862944 * jax.random.uniform(splits[6], (4, FINE), jnp.float32) ** levels(splits[6], (4, FINE), ((1, 32),), -0.2, 0.2)), 0.5, 2.0)
    derivative = noise(splits[7], (3, NODES, NODES), NODES ** -0.5, 1.0, (), jnp.float32)
    lift = noise(splits[8], (4, NODES, FACE_NODES), FACE_NODES ** -0.5, 1.5, (), jnp.float32)
    prolong = noise(splits[9], (CHILDREN, NODES, PMODES), PMODES ** -0.5, 2.0, (), jnp.float32)
    coarse_step = noise(splits[10], (BLOCK, COARSE), 1.0, 6.0, ((1, 32),), jnp.float32)
    reg_weight = jnp.clip(jnp.exp(math.log(10.0) - 2.3025851 * jax.random.uniform(splits[11], (BLOCK, COARSE), jnp.float32) ** levels(splits[11], (BLOCK, COARSE), ((1, 32),), -0.2, 0.2)), 1.0, 10.0)
    observe = jnp.clip(jnp.exp(math.log(1.0) - 2.3025851 * jax.random.uniform(splits[12], (NODES, FINE), jnp.float32) ** levels(splits[12], (NODES, FINE), ((1, 32),), -0.2, 0.2)), 0.1, 1.0)
    owner_keys = jax.random.split(jax.random.fold_in(splits[13], 1), FINE // E_DEV)
    owner_turns = jax.random.permutation(jax.random.fold_in(splits[13], 3), FINE // E_DEV)
    owner = jax.vmap(lambda own, number: routed_block(jax.random.fold_in(splits[13], 2), own, number, E_DEV, DEVICES, 1, CAP, 2))(owner_keys, owner_turns).reshape((FINE, 1))
    coarse_local = place_ends(jax.random.randint(splits[14], (FINE,), 0, CB_DEV), jax.random.fold_in(splits[14], 1), 0, CB_DEV - 1).astype(jnp.int32)
    child = place_ends(jax.random.randint(splits[15], (FINE,), 0, CHILDREN), jax.random.fold_in(splits[15], 1), 0, CHILDREN - 1).astype(jnp.int32)
    neighbor = place_ends(jax.random.randint(splits[16], (4, FINE), 0, TABLE), jax.random.fold_in(splits[16], 1), 0, TABLE - 1).astype(jnp.int32)
    orient = place_ends(jax.random.randint(splits[17], (4, FINE), 0, 6), jax.random.fold_in(splits[17], 1), 0, 5).astype(jnp.int32)
    send_face = place_ends(jax.random.randint(splits[18], (SENT,), 0, 4 * E_DEV), jax.random.fold_in(splits[18], 1), 0, (4 * E_DEV) - 1).astype(jnp.int32)
    return dict(state0=state0, delta=delta, adjoint=adjoint, model=model, geometry=geometry, normals=normals, face_scale=face_scale, derivative=derivative, lift=lift, prolong=prolong, coarse_step=coarse_step, reg_weight=reg_weight, observe=observe, owner=owner, coarse_local=coarse_local, child=child, neighbor=neighbor, orient=orient, send_face=send_face)


time_step = 0.2
penalty = 0.5
stress_of = ((0, 5, 4), (5, 1, 3), (4, 3, 2))
voigt_pairs = ((0, 0), (1, 1), (2, 2), (1, 2), (0, 2), (0, 1))
stress_diag = (1.0, 1.0, 1.0, 0.0, 0.0, 0.0)


def tables():
    triangle = [(along_one, along_two) for along_one in range(5) for along_two in range(5 - along_one)]
    volume_nodes = [(along_one, along_two, along_three) for along_one in range(5) for along_two in range(5 - along_one) for along_three in range(5 - along_one - along_two)]
    face_index = np.zeros((15, 4), np.int32)
    for entry_pos, pair_ab in enumerate(triangle):
        places = [(pair_ab[0], pair_ab[1], 0), (pair_ab[0], 0, pair_ab[1]), (0, pair_ab[0], pair_ab[1]), (pair_ab[0], pair_ab[1], 4 - pair_ab[0] - pair_ab[1])]
        for face_id, node_key in enumerate(places):
            face_index[entry_pos, face_id] = volume_nodes.index(node_key)
    orders = [(0, 1, 2), (1, 2, 0), (2, 0, 1), (0, 2, 1), (2, 1, 0), (1, 0, 2)]
    turning = np.zeros((6, 15), np.int32)
    for orient_id, ordering in enumerate(orders):
        for entry_pos, pair_ab in enumerate(triangle):
            coords = (pair_ab[0], pair_ab[1], 4 - pair_ab[0] - pair_ab[1])
            turning[orient_id, entry_pos] = triangle.index((coords[ordering[0]], coords[ordering[1]]))
    return face_index, turning


def pick_traces(field, chosen, face_index):
    elements = field.shape[2]
    face_ids = chosen // elements
    elem_ids = chosen % elements
    return field[:, jnp.asarray(face_index)[:, face_ids], elem_ids[None, :]]


def operator_terms(field, remote, neighbor, orient, geometry, normals, face_scale, derivative, lift, face_index, turning, with_penalty):
    elements = field.shape[2]
    highest = lax.Precision.HIGHEST
    inner = field[:, face_index, :].reshape(9, 15, 4 * elements)
    table = jnp.concatenate([inner, remote], axis=2)
    outer = table[:, :, neighbor.reshape(-1)]
    rotate = jnp.asarray(turning)[orient.reshape(-1)].T
    outer = jnp.take_along_axis(outer, rotate[None, :, :], axis=1)
    jump = (outer - inner).reshape(9, 15, 4, elements)
    local_grad = jnp.einsum("knm,cme->ckne", derivative, field, precision=highest)
    physical = jnp.einsum("ike,ckne->cine", geometry.reshape(3, 3, elements), local_grad, precision=highest)
    half_scale = 0.5 * face_scale[None, :, :]
    channels = []
    for row_id in range(3):
        channels.append(half_scale * sum(normals[col_id][None] * jump[3 + stress_of[row_id][col_id]] for col_id in range(3)))
    channels.append(half_scale * sum(normals[col_id][None] * jump[col_id] for col_id in range(3)))
    for pair_ij in voigt_pairs:
        channels.append(half_scale * (normals[pair_ij[0]][None] * jump[pair_ij[1]] + normals[pair_ij[1]][None] * jump[pair_ij[0]]))
    if with_penalty:
        for comp_id in range(9):
            channels.append(penalty * face_scale[None, :, :] * jump[comp_id])
    lifted = jnp.einsum("fnm,cmfe->cne", lift, jnp.stack(channels), precision=highest)
    terms_b = jnp.stack([sum(physical[3 + stress_of[row_id][col_id], col_id] for col_id in range(3)) + lifted[row_id] for row_id in range(3)])
    terms_lam = sum(physical[col_id, col_id] for col_id in range(3)) + lifted[3]
    terms_mu = jnp.stack([physical[pair_ij[1], pair_ij[0]] + physical[pair_ij[0], pair_ij[1]] + lifted[4 + voigt_id] for voigt_id, pair_ij in enumerate(voigt_pairs)])
    pen_terms = lifted[10:19] if with_penalty else None
    return terms_b, terms_lam, terms_mu, pen_terms


def apply_model(params, terms_b, terms_lam, terms_mu):
    velocity = params[0][None] * terms_b
    diagonal = jnp.asarray(stress_diag, jnp.float32)[:, None, None]
    stress = params[2][None] * terms_mu + diagonal * (params[1] * terms_lam)[None]
    return jnp.concatenate([velocity, stress], axis=0)


def section(state0, delta, adjoint, model, geometry, normals, face_scale, observe, neighbor, orient, remote_state, remote_delta, remote_adjoint, fetched, child, derivative, lift, prolong, face_index, turning):
    elements = state0.shape[2]
    highest = lax.Precision.HIGHEST
    shapes = prolong[child]
    step_fine = jnp.einsum("enk,pke->pne", shapes, fetched.reshape(3, -1, elements), precision=highest)
    base = operator_terms(state0, remote_state, neighbor, orient, geometry, normals, face_scale, derivative, lift, face_index, turning, False)
    moved = operator_terms(delta, remote_delta, neighbor, orient, geometry, normals, face_scale, derivative, lift, face_index, turning, True)
    backed = operator_terms(adjoint, remote_adjoint, neighbor, orient, geometry, normals, face_scale, derivative, lift, face_index, turning, True)
    delta_next = delta + time_step * (apply_model(model, moved[0], moved[1], moved[2]) + moved[3] + apply_model(step_fine, base[0], base[1], base[2]))
    adjoint_next = adjoint + time_step * (apply_model(model, backed[0], backed[1], backed[2]) + backed[3] + observe[None] * delta_next)
    grad_b = time_step * jnp.sum(adjoint_next[0:3] * base[0], axis=0)
    grad_lam = time_step * jnp.sum(adjoint_next[3:6], axis=0) * base[1]
    grad_mu = time_step * jnp.sum(adjoint_next[3:9] * base[2], axis=0)
    fine_grad = jnp.stack([grad_b, grad_lam, grad_mu])
    restricted = jnp.einsum("enk,pne->pke", shapes, fine_grad, precision=highest).reshape(-1, elements)
    return delta_next, adjoint_next, restricted


def reference(state0, delta, adjoint, model, geometry, normals, face_scale, derivative, lift, prolong, coarse_step, reg_weight, observe, owner, coarse_local, child, neighbor, orient, send_face):
    face_index, turning = tables()

    def per_device(array):
        return jnp.moveaxis(array.reshape(array.shape[:-1] + (DEVICES, E_DEV)), -2, 0)

    def to_whole(array):
        moved = jnp.moveaxis(array, 0, -2)
        return moved.reshape(moved.shape[:-2] + (FINE,))

    chosen = send_face.reshape(DEVICES, N_WAVE * CAPF)

    def received(field):
        sent = jax.vmap(lambda one_field, one_list: pick_traces(one_field, one_list, face_index))(per_device(field), chosen)
        sent = sent.reshape(N_REGION, N_WAVE, 9, 15, N_WAVE, CAPF)
        return jnp.transpose(sent, (0, 4, 2, 3, 1, 5)).reshape(DEVICES, 9, 15, N_WAVE * CAPF)

    global_ids = (owner[:, 0] * CB_DEV + coarse_local).astype(jnp.int32)
    fetched = coarse_step[:, global_ids]
    inputs = (per_device(state0), per_device(delta), per_device(adjoint), per_device(model), per_device(geometry), per_device(normals), per_device(face_scale), per_device(observe), per_device(neighbor), per_device(orient), received(state0), received(delta), received(adjoint), per_device(fetched), per_device(child))

    def run_one(pack):
        return section(pack[0], pack[1], pack[2], pack[3], pack[4], pack[5], pack[6], pack[7], pack[8], pack[9], pack[10], pack[11], pack[12], pack[13], pack[14], derivative, lift, prolong, face_index, turning)

    delta_dev, adjoint_dev, restricted_dev = lax.map(run_one, inputs)
    restricted = to_whole(restricted_dev)
    summed = jax.ops.segment_sum(restricted.T, global_ids, num_segments=COARSE).T
    hess_vec = summed + reg_weight * coarse_step
    return to_whole(delta_dev), to_whole(adjoint_dev), hess_vec
```

```python
import functools
import jax
import jax.numpy as jnp
import numpy as np
from jax import lax
from jax.experimental import pallas as pl
from jax.experimental.pallas import tpu as pltpu
from jax.sharding import PartitionSpec as P

time_step = 0.2
penalty = 0.5
stress_of = ((0, 5, 4), (5, 1, 3), (4, 3, 2))
voigt_pairs = ((0, 0), (1, 1), (2, 2), (1, 2), (0, 2), (0, 1))
F32 = jnp.float32
BF16 = jnp.bfloat16
NODES, FACE, ROWS = 35, 15, 27 * 16
VROW = 40
KROW = 48


def tables():
    triangle = [(one, two) for one in range(5) for two in range(5 - one)]
    volume_nodes = [
        (one, two, three)
        for one in range(5)
        for two in range(5 - one)
        for three in range(5 - one - two)
    ]
    face_index = np.zeros((15, 4), np.int32)
    for entry, (a, b) in enumerate(triangle):
        for face, key in enumerate([(a, b, 0), (a, 0, b), (0, a, b), (a, b, 4 - a - b)]):
            face_index[entry, face] = volume_nodes.index(key)
    orders = [(0, 1, 2), (1, 2, 0), (2, 0, 1), (0, 2, 1), (2, 1, 0), (1, 0, 2)]
    turning = np.zeros((6, 15), np.int32)
    for orient_id, order in enumerate(orders):
        for entry, (a, b) in enumerate(triangle):
            coords = (a, b, 4 - a - b)
            turning[orient_id, entry] = triangle.index((coords[order[0]], coords[order[1]]))
    return face_index, turning


def split(x):
    high = x.astype(BF16)
    low = (x - high.astype(F32)).astype(BF16)
    return high, low


def dot(a, b):
    return jnp.dot(a, b, preferred_element_type=F32)


def dot_nt(a, b):
    return lax.dot_general(a, b, (((1,), (1,)), ((), ())), preferred_element_type=F32)


def pad_rows(x, rows):
    return jnp.concatenate([x, jnp.zeros((rows - x.shape[0],) + x.shape[1:], x.dtype)], axis=0)


def one_hot(ids, count, start=0):
    rows = lax.broadcasted_iota(jnp.int32, (count, ids.shape[1]), 0) + start
    return jnp.where(rows == ids, 1.0, 0.0).astype(BF16)


def turn_rows(turning, orient_row):
    lanes = orient_row.shape[1]
    rows = lax.broadcasted_iota(jnp.int32, (16, lanes), 0)
    result = rows
    for orient_id in range(1, 6):
        table = jnp.zeros((16, lanes), jnp.int32)
        for m in range(15):
            table = jnp.where(rows == m, int(turning[orient_id, m]), table)
        result = jnp.where(orient_row == orient_id, table, result)
    return result


def rotate(x, index):
    first, second = x[0:8], x[8:16]
    halves = []
    for h in range(2):
        part = index[8 * h : 8 * h + 8]
        inside = part & 7
        a = jnp.take_along_axis(first, inside, axis=0)
        b = jnp.take_along_axis(second, inside, axis=0)
        halves.append(jnp.where(part < 8, a, b))
    return jnp.concatenate(halves, axis=0)


def send_kernel(q0_ref, q1_ref, q2_ref, select_ref, send_ref, high_ref, low_ref, sent_ref):
    elements = q0_ref.shape[2]
    select = select_ref[...]
    for s, ref in enumerate((q0_ref, q1_ref, q2_ref)):
        for c in range(9):
            high, low = split(pad_rows(ref[c], KROW))
            trace = dot(select, jnp.concatenate([high, low], axis=0))
            t_high, t_low = split(trace)
            row = (s * 9 + c) * 16
            for f in range(4):
                high_ref[row : row + 16, f * elements : (f + 1) * elements] = t_high[
                    16 * f : 16 * f + 16
                ]
                low_ref[row : row + 16, f * elements : (f + 1) * elements] = t_low[
                    16 * f : 16 * f + 16
                ]
    picked = one_hot(send_ref[...], 4 * elements)
    sent = dot(high_ref[...], picked) + dot(low_ref[...], picked)
    sent_ref[...] = sent.T


def spread_kernel(coarse_ref, out_ref):
    width = coarse_ref.shape[1]
    rows = out_ref.shape[1]
    padded = pad_rows(coarse_ref[...], 4 * rows)
    for s in range(rows):
        for j in range(4):
            row = padded[4 * s + j : 4 * s + j + 1]
            out_ref[:, s, j * width : (j + 1) * width] = jnp.broadcast_to(
                row, (out_ref.shape[0], width)
            )


def own_kernel(
    turning,
    q0_ref,
    q1_ref,
    q2_ref,
    model_ref,
    geometry_ref,
    neighbor_ref,
    orient_ref,
    derivative_ref,
    lift_ref,
    prolong_ref,
    high_ref,
    low_ref,
    own_ref,
    vol0_ref,
    vol1_ref,
    vol2_ref,
    lift_out,
    prolong_out,
    restrict_out,
    left_ref,
    rows_ref,
):
    elements = q0_ref.shape[2]
    left_ref[...] = jnp.zeros_like(left_ref)
    for k in range(3):
        high, low = split(derivative_ref[k])
        r = k * VROW
        left_ref[r : r + NODES, 0:NODES] = high.astype(F32)
        left_ref[r : r + NODES, KROW : KROW + NODES] = high.astype(F32)
        left_ref[r : r + NODES, 2 * KROW : 2 * KROW + NODES] = low.astype(F32)
    left = left_ref[...].astype(BF16)
    rows_ref[...] = jnp.zeros_like(rows_ref)
    for f in range(4):
        rows_ref[16 * f : 16 * f + FACE, 0:NODES] = lift_ref[:, f, :]
    turned = rows_ref[...].T
    high, low = split(turned[0:VROW, 0:64])
    lift_out[...] = jnp.concatenate([high, high, low], axis=1)
    rows_ref[...] = jnp.zeros_like(rows_ref)
    rows_ref[0:80, 0:NODES] = prolong_ref[...].reshape(80, NODES)
    plain = rows_ref[...]
    high, low = split(plain[0:80, 0:KROW])
    restrict_out[...] = jnp.concatenate([high, high, low], axis=1)
    turned = plain.T
    high, low = split(turned[0:VROW, 0:80])
    prolong_out[...] = jnp.concatenate([high, high, low], axis=1)

    geometry = geometry_ref[...]
    for s, (ref, out) in enumerate(
        ((q0_ref, vol0_ref), (q1_ref, vol1_ref), (q2_ref, vol2_ref))
    ):
        local = []
        for c in range(9):
            high, low = split(pad_rows(ref[c], KROW))
            local.append(dot(left, jnp.concatenate([high, low, high], axis=0)))

        def grad(c, i):
            total = None
            for k in range(3):
                term = geometry[3 * i + k : 3 * i + k + 1] * local[c][k * VROW : k * VROW + VROW]
                total = term if total is None else total + term
            return total[0:NODES]

        terms = []
        for i in range(3):
            terms.append(sum(grad(3 + stress_of[i][j], j) for j in range(3)))
        for i, j in voigt_pairs:
            terms.append(2.0 * grad(i, i) if i == j else grad(j, i) + grad(i, j))
        if s == 0:
            for c in range(9):
                out[c] = terms[c]
        else:
            trace = (0.5 * model_ref[1]) * (terms[3] + terms[4] + terms[5])
            for c in range(9):
                value = (model_ref[0] if c < 3 else model_ref[2]) * terms[c]
                if 3 <= c < 6:
                    value = value + trace
                out[c] = ref[c] + time_step * value

    for f in range(4):
        lanes = slice(f * elements, (f + 1) * elements)
        picked = one_hot(neighbor_ref[f : f + 1], 4 * elements)
        outer = dot(high_ref[...], picked) + dot(low_ref[...], picked)
        index = turn_rows(turning, orient_ref[f : f + 1])
        for cs in range(27):
            r = slice(16 * cs, 16 * cs + 16)
            inner = high_ref[r, lanes].astype(F32) + low_ref[r, lanes].astype(F32)
            own_ref[r, lanes] = rotate(outer[r], index) - inner


def join_kernel(
    turning,
    recv_ref,
    coarse_ref,
    neighbor_ref,
    orient_ref,
    own_ref,
    vol0_ref,
    vol1_ref,
    vol2_ref,
    lift_ref,
    prolong_ref,
    restrict_ref,
    model_ref,
    normals_ref,
    scale_ref,
    observe_ref,
    owner_ref,
    local_ref,
    child_ref,
    delta_ref,
    adjoint_ref,
    message_ref,
    jump_ref,
    spread_ref,
):
    elements = model_ref.shape[2]
    devices = coarse_ref.shape[0]
    width = coarse_ref.shape[2] // 4
    slots = recv_ref.shape[0]
    received = recv_ref[...].T
    high, low = split(received)
    received = jnp.concatenate([high, low], axis=1)
    for f in range(4):
        lanes = slice(f * elements, (f + 1) * elements)
        picked = one_hot(neighbor_ref[f : f + 1], slots, 4 * elements)
        outer = dot(received, jnp.concatenate([picked, picked], axis=0))
        index = turn_rows(turning, orient_ref[f : f + 1])
        for cs in range(27):
            r = slice(16 * cs, 16 * cs + 16)
            jump_ref[r, lanes] = own_ref[r, lanes] + rotate(outer[r], index)

    owner_hot = one_hot(owner_ref[...], devices)
    local_hot = jnp.where(
        lax.broadcasted_iota(jnp.int32, (width, elements), 0) == local_ref[...], 1.0, 0.0
    )
    child_hot = jnp.where(
        lax.broadcasted_iota(jnp.int32, (8, elements), 0) == child_ref[...], 1.0, 0.0
    )
    fetched = []
    for s in range(coarse_ref.shape[1]):
        high, low = split(coarse_ref[:, s, :].T)
        spread = dot(high, owner_hot) + dot(low, owner_hot)
        for j in range(4):
            block = spread[j * width : (j + 1) * width] * local_hot
            fetched.append(jnp.sum(block, axis=0, keepdims=True))
    prolong = prolong_ref[...]
    step_fine = []
    for p in range(3):
        masked = jnp.concatenate([fetched[10 * p + k] * child_hot for k in range(10)], axis=0)
        high, low = split(masked)
        step_fine.append(
            dot(prolong, jnp.concatenate([high, low, high], axis=0))[0:NODES]
        )

    lift = lift_ref[...]

    def lifted(pieces):
        high, low = split(jnp.concatenate(pieces, axis=0))
        return dot(lift, jnp.concatenate([high, low, high], axis=0))[0:NODES]

    def flux(s):
        scaled, normal = [], []
        for f in range(4):
            half = 0.5 * scale_ref[f : f + 1]
            scaled.append(half)
            normal.append([half * normals_ref[j, f : f + 1] for j in range(3)])

        def jump(c, f):
            r = (s * 9 + c) * 16
            return jump_ref[r : r + 16, f * elements : (f + 1) * elements]

        result = []
        for i in range(3):
            result.append(
                lifted(
                    [
                        sum(normal[f][j] * jump(3 + stress_of[i][j], f) for j in range(3))
                        for f in range(4)
                    ]
                )
            )
        for i, j in voigt_pairs:
            if i == j:
                result.append(lifted([(2.0 * normal[f][i]) * jump(i, f) for f in range(4)]))
            else:
                result.append(
                    lifted(
                        [
                            normal[f][i] * jump(j, f) + normal[f][j] * jump(i, f)
                            for f in range(4)
                        ]
                    )
                )
        if s == 0:
            return result, None
        return result, [lifted([scaled[f] * jump(c, f) for f in range(4)]) for c in range(9)]

    def apply(first, second, third, terms):
        trace = (0.5 * second) * (terms[3] + terms[4] + terms[5])
        values = []
        for c in range(9):
            value = (first if c < 3 else third) * terms[c]
            values.append(value + trace if 3 <= c < 6 else value)
        return values

    lift0, _ = flux(0)
    base = [vol0_ref[c] + lift0[c] for c in range(9)]
    terms, pen = flux(1)
    moved = apply(model_ref[0], model_ref[1], model_ref[2], terms)
    pushed = apply(step_fine[0], step_fine[1], step_fine[2], base)
    for c in range(9):
        delta_ref[c] = vol1_ref[c] + time_step * (moved[c] + pen[c] + pushed[c])
    terms, pen = flux(2)
    moved = apply(model_ref[0], model_ref[1], model_ref[2], terms)
    for c in range(9):
        adjoint_ref[c] = vol2_ref[c] + time_step * (
            moved[c] + pen[c] + observe_ref[...] * delta_ref[c]
        )
    grads = [
        time_step * sum(adjoint_ref[i] * base[i] for i in range(3)),
        (0.5 * time_step)
        * ((adjoint_ref[3] + adjoint_ref[4] + adjoint_ref[5]) * (base[3] + base[4] + base[5])),
        time_step * sum(adjoint_ref[c] * base[c] for c in range(3, 9)),
    ]
    owner_twice = jnp.concatenate([owner_hot, owner_hot], axis=1)
    spread_ref[...] = jnp.zeros_like(spread_ref)
    for p in range(3):
        high, low = split(pad_rows(grads[p], KROW))
        parts = dot(restrict_ref[...], jnp.concatenate([high, low, high], axis=0))
        for k in range(10):
            row = jnp.sum(parts[8 * k : 8 * k + 8] * child_hot, axis=0, keepdims=True)
            high, low = split(row * local_hot)
            at = (10 * p + k) * width
            spread_ref[at : at + width] = jnp.concatenate([high, low], axis=1)
    gathered = dot_nt(owner_twice, spread_ref[...])
    for s in range(message_ref.shape[1]):
        message_ref[:, s, :] = gathered[:, s * 4 * width : (s + 1) * 4 * width]


def sum_kernel(arrived_ref, reg_ref, coarse_ref, out_ref):
    width = coarse_ref.shape[1]
    total = jnp.sum(arrived_ref[...], axis=0)
    weighted = reg_ref[...] * coarse_ref[...]
    for row in range(coarse_ref.shape[0]):
        s, j = row // 4, row % 4
        out_ref[row : row + 1] = (
            total[s : s + 1, j * width : (j + 1) * width] + weighted[row : row + 1]
        )


def call(kernel, outs, scratch=(), name=None, flops=0, bytes_accessed=0):
    return pl.pallas_call(
        kernel,
        out_shape=outs,
        scratch_shapes=list(scratch),
        name=name,
        cost_estimate=pl.CostEstimate(
            flops=flops, bytes_accessed=bytes_accessed, transcendentals=0
        ),
    )


def body(
    state0,
    delta,
    adjoint,
    model,
    geometry,
    normals,
    face_scale,
    derivative,
    lift,
    prolong,
    coarse_step,
    reg_weight,
    observe,
    owner,
    coarse_local,
    child,
    neighbor,
    orient,
    send_face,
):
    face_index, turning = tables()
    elements = state0.shape[2]
    wave_size = lax.axis_size("wave")
    devices = lax.axis_size(("region", "wave"))
    sends = send_face.shape[0]
    block, width = coarse_step.shape
    packs = 8
    everyone = ("region", "wave")
    select = np.zeros((64, 2 * KROW), np.float32)
    for f in range(4):
        for m in range(FACE):
            select[16 * f + m, face_index[m, f]] = 1.0
            select[16 * f + m, KROW + face_index[m, f]] = 1.0
    shape = jax.ShapeDtypeStruct

    spread = call(spread_kernel, shape((devices, packs, 4 * width), F32), name="spread")(coarse_step)
    high, low, sent = call(
        send_kernel,
        (
            shape((ROWS, 4 * elements), BF16),
            shape((ROWS, 4 * elements), BF16),
            shape((sends, ROWS), F32),
        ),
        name="send",
        bytes_accessed=3 << 20,
        flops=1 << 28,
    )(state0, delta, adjoint, jnp.asarray(select, BF16), send_face.reshape(1, sends))
    coarse = lax.all_to_all(spread, everyone, split_axis=0, concat_axis=0, tiled=True)
    got = lax.all_to_all(
        sent.reshape(wave_size, sends // wave_size, ROWS),
        "wave",
        split_axis=0,
        concat_axis=0,
        tiled=True,
    ).reshape(sends, ROWS)
    state = shape((9, NODES, elements), F32)
    own, vol0, vol1, vol2, lift_left, prolong_left, restrict_left = call(
        functools.partial(own_kernel, turning),
        (
            shape((ROWS, 4 * elements), F32),
            state,
            state,
            state,
            shape((VROW, 192), BF16),
            shape((VROW, 240), BF16),
            shape((80, 3 * KROW), BF16),
        ),
        scratch=(pltpu.VMEM((3 * VROW, 3 * KROW), F32), pltpu.VMEM((128, 128), F32)),
        name="own",
        bytes_accessed=8 << 20,
        flops=1 << 32,
    )(
        state0,
        delta,
        adjoint,
        model,
        geometry,
        neighbor,
        orient,
        derivative,
        lift.transpose(2, 0, 1),
        prolong.transpose(2, 0, 1),
        high,
        low,
    )
    delta_next, adjoint_next, message = call(
        functools.partial(join_kernel, turning),
        (state, state, shape((devices, packs, 4 * width), F32)),
        scratch=(
            pltpu.VMEM((ROWS, 4 * elements), F32),
            pltpu.VMEM((packs * 4 * width, 2 * elements), BF16),
        ),
        name="join",
        bytes_accessed=8 << 20,
        flops=1 << 30,
    )(
        got,
        coarse,
        neighbor,
        orient,
        own,
        vol0,
        vol1,
        vol2,
        lift_left,
        prolong_left,
        restrict_left,
        model,
        normals,
        face_scale,
        observe,
        owner.reshape(1, elements),
        coarse_local.reshape(1, elements),
        child.reshape(1, elements),
    )
    arrived = lax.all_to_all(message, everyone, split_axis=0, concat_axis=0, tiled=True)
    hess_vec = call(sum_kernel, shape((block, width), F32), name="total")(
        arrived, reg_weight, coarse_step
    )
    return (delta_next, adjoint_next, hess_vec)


def solution(mesh):
    both = ("region", "wave")
    wide, flat = P(None, None, both), P(None, both)
    placed = (
        wide,
        wide,
        wide,
        wide,
        flat,
        wide,
        flat,
        P(),
        P(),
        P(),
        flat,
        flat,
        flat,
        P(both, None),
        P(both),
        P(both),
        flat,
        flat,
        P(both),
    )
    return jax.shard_map(
        body, mesh=mesh, in_specs=placed, out_specs=(wide, wide, flat), check_vma=False
    )
```

```python
import functools
import jax
import jax.numpy as jnp
import numpy as np
from jax import lax
from jax.experimental import pallas as pl
from jax.experimental.pallas import tpu as pltpu
from jax.sharding import PartitionSpec as P

time_step = 0.2
penalty = 0.5
stress_of = ((0, 5, 4), (5, 1, 3), (4, 3, 2))
voigt_pairs = ((0, 0), (1, 1), (2, 2), (1, 2), (0, 2), (0, 1))
F32 = jnp.float32
BF16 = jnp.bfloat16
NODES, FACE, ROWS = 35, 15, 27 * 16
VROW = 40
KROW = 48


def tables():
    triangle = [(one, two) for one in range(5) for two in range(5 - one)]
    volume_nodes = [
        (one, two, three)
        for one in range(5)
        for two in range(5 - one)
        for three in range(5 - one - two)
    ]
    face_index = np.zeros((15, 4), np.int32)
    for entry, (a, b) in enumerate(triangle):
        for face, key in enumerate([(a, b, 0), (a, 0, b), (0, a, b), (a, b, 4 - a - b)]):
            face_index[entry, face] = volume_nodes.index(key)
    orders = [(0, 1, 2), (1, 2, 0), (2, 0, 1), (0, 2, 1), (2, 1, 0), (1, 0, 2)]
    turning = np.zeros((6, 15), np.int32)
    for orient_id, order in enumerate(orders):
        for entry, (a, b) in enumerate(triangle):
            coords = (a, b, 4 - a - b)
            turning[orient_id, entry] = triangle.index((coords[order[0]], coords[order[1]]))
    return face_index, turning


def split(x):
    high = x.astype(BF16)
    low = (x - high.astype(F32)).astype(BF16)
    return high, low


def dot(a, b):
    return jnp.dot(a, b, preferred_element_type=F32)


def dot_nt(a, b):
    return lax.dot_general(a, b, (((1,), (1,)), ((), ())), preferred_element_type=F32)


def pad_rows(x, rows):
    return jnp.concatenate([x, jnp.zeros((rows - x.shape[0],) + x.shape[1:], x.dtype)], axis=0)


def one_hot(ids, count, start=0):
    rows = lax.broadcasted_iota(jnp.int32, (count, ids.shape[1]), 0) + start
    return jnp.where(rows == ids, 1.0, 0.0).astype(BF16)


def turn_rows(turning, orient_row):
    lanes = orient_row.shape[1]
    rows = lax.broadcasted_iota(jnp.int32, (16, lanes), 0)
    result = rows
    for orient_id in range(1, 6):
        table = jnp.zeros((16, lanes), jnp.int32)
        for m in range(15):
            table = jnp.where(rows == m, int(turning[orient_id, m]), table)
        result = jnp.where(orient_row == orient_id, table, result)
    return result


def rotate(x, index):
    first, second = x[0:8], x[8:16]
    halves = []
    for h in range(2):
        part = index[8 * h : 8 * h + 8]
        inside = part & 7
        a = jnp.take_along_axis(first, inside, axis=0)
        b = jnp.take_along_axis(second, inside, axis=0)
        halves.append(jnp.where(part < 8, a, b))
    return jnp.concatenate(halves, axis=0)


def fetch(pairs, sems):
    copies = []
    for index, (source, target) in enumerate(pairs):
        copy = pltpu.make_async_copy(source, target, sems.at[index])
        copy.start()
        copies.append(copy)
    return copies


def send_kernel(
    q0_hbm,
    q1_hbm,
    q2_hbm,
    select_hbm,
    send_hbm,
    coarse_hbm,
    high_out,
    low_out,
    sent_ref,
    q_ref,
    select_ref,
    send_ref,
    coarse_ref,
    high_ref,
    low_ref,
    in_sems,
    out_sems,
):
    elements = q_ref.shape[3]
    slots = sent_ref.shape[1]
    block, width = coarse_ref.shape
    sources = (q0_hbm, q1_hbm, q2_hbm)
    copies = fetch(
        [(select_hbm, select_ref)]
        + [(sources[s], q_ref.at[s]) for s in range(3)]
        + [(send_hbm, send_ref), (coarse_hbm, coarse_ref)],
        in_sems,
    )
    copies[0].wait()
    select = select_ref[...]
    written = []
    for s in range(3):
        copies[1 + s].wait()
        for c in range(9):
            high, low = split(pad_rows(q_ref[s, c], KROW))
            trace = dot(select, jnp.concatenate([high, low], axis=0))
            t_high, t_low = split(trace)
            row = (s * 9 + c) * 16
            for f in range(4):
                lanes = slice(f * elements, (f + 1) * elements)
                high_ref[row : row + 16, lanes] = t_high[16 * f : 16 * f + 16]
                low_ref[row : row + 16, lanes] = t_low[16 * f : 16 * f + 16]
        rows = pl.ds(s * 144, 144)
        written += fetch(
            [(high_ref.at[rows], high_out.at[rows]), (low_ref.at[rows], low_out.at[rows])],
            out_sems.at[s],
        )
    copies[4].wait()
    picked = one_hot(send_ref[...], 4 * elements)
    sent = dot(high_ref[...], picked) + dot(low_ref[...], picked)
    sent_ref[:, :, 0:ROWS] = sent.T.reshape(sent_ref.shape[0], slots, ROWS)
    copies[5].wait()
    pieces = spare(block, slots)
    padded = pad_rows(coarse_ref[...], pieces * slots)
    for h in range(pieces):
        part = padded[h * slots : (h + 1) * slots]
        for w in range(sent_ref.shape[0]):
            sent_ref[w, :, ROWS + h * width : ROWS + (h + 1) * width] = part
    for copy in written:
        copy.wait()


def spare(block, slots):
    return -(-block // slots)


def pick_kernel(got_ref, out_ref):
    waves, slots, _ = got_ref.shape
    rows = out_ref.shape[0]
    width = out_ref.shape[1] // waves
    for w in range(waves):
        for h in range(rows // slots):
            out_ref[h * slots : (h + 1) * slots, w * width : (w + 1) * width] = got_ref[
                w, :, ROWS + h * width : ROWS + (h + 1) * width
            ]


def own_kernel(
    turning,
    q0_ref,
    q1_ref,
    q2_ref,
    model_ref,
    geometry_ref,
    neighbor_ref,
    orient_ref,
    derivative_ref,
    lift_ref,
    prolong_ref,
    high_ref,
    low_ref,
    own_ref,
    vol0_ref,
    vol1_ref,
    vol2_ref,
    lift_out,
    prolong_out,
    restrict_out,
    left_ref,
    rows_ref,
):
    elements = q0_ref.shape[2]
    left_ref[...] = jnp.zeros_like(left_ref)
    for k in range(3):
        high, low = split(derivative_ref[k])
        r = k * VROW
        left_ref[r : r + NODES, 0:NODES] = high.astype(F32)
        left_ref[r : r + NODES, KROW : KROW + NODES] = high.astype(F32)
        left_ref[r : r + NODES, 2 * KROW : 2 * KROW + NODES] = low.astype(F32)
    left = left_ref[...].astype(BF16)
    rows_ref[...] = jnp.zeros_like(rows_ref)
    for f in range(4):
        rows_ref[16 * f : 16 * f + FACE, 0:NODES] = lift_ref[:, f, :]
    turned = rows_ref[...].T
    high, low = split(turned[0:VROW, 0:64])
    lift_out[...] = jnp.concatenate([high, high, low], axis=1)
    rows_ref[...] = jnp.zeros_like(rows_ref)
    rows_ref[0:80, 0:NODES] = prolong_ref[...].reshape(80, NODES)
    plain = rows_ref[...]
    high, low = split(plain[0:80, 0:KROW])
    restrict_out[...] = jnp.concatenate([high, high, low], axis=1)
    turned = plain.T
    high, low = split(turned[0:VROW, 0:80])
    prolong_out[...] = jnp.concatenate([high, high, low], axis=1)

    geometry = geometry_ref[...]
    for s, (ref, out) in enumerate(
        ((q0_ref, vol0_ref), (q1_ref, vol1_ref), (q2_ref, vol2_ref))
    ):
        local = []
        for c in range(9):
            high, low = split(pad_rows(ref[c], KROW))
            local.append(dot(left, jnp.concatenate([high, low, high], axis=0)))

        def grad(c, i):
            total = None
            for k in range(3):
                term = geometry[3 * i + k : 3 * i + k + 1] * local[c][k * VROW : k * VROW + VROW]
                total = term if total is None else total + term
            return total[0:NODES]

        terms = []
        for i in range(3):
            terms.append(sum(grad(3 + stress_of[i][j], j) for j in range(3)))
        for i, j in voigt_pairs:
            terms.append(2.0 * grad(i, i) if i == j else grad(j, i) + grad(i, j))
        if s == 0:
            for c in range(9):
                out[c] = terms[c]
        else:
            trace = (0.5 * model_ref[1]) * (terms[3] + terms[4] + terms[5])
            for c in range(9):
                value = (model_ref[0] if c < 3 else model_ref[2]) * terms[c]
                if 3 <= c < 6:
                    value = value + trace
                out[c] = ref[c] + time_step * value

    for f in range(4):
        lanes = slice(f * elements, (f + 1) * elements)
        picked = one_hot(neighbor_ref[f : f + 1], 4 * elements)
        outer = dot(high_ref[...], picked) + dot(low_ref[...], picked)
        index = turn_rows(turning, orient_ref[f : f + 1])
        for cs in range(27):
            r = slice(16 * cs, 16 * cs + 16)
            inner = high_ref[r, lanes].astype(F32) + low_ref[r, lanes].astype(F32)
            own_ref[r, lanes] = rotate(outer[r], index) - inner


def model_terms(first, second, third, terms):
    trace = (0.5 * second) * (terms[3] + terms[4] + terms[5])
    values = []
    for c in range(9):
        value = (first if c < 3 else third) * terms[c]
        values.append(value + trace if 3 <= c < 6 else value)
    return values


def jump_kernel(
    turning,
    got_ref,
    neighbor_hbm,
    orient_hbm,
    own_ref,
    lift_ref,
    normals_hbm,
    scale_hbm,
    vol0_ref,
    vol1_ref,
    vol2_ref,
    model_hbm,
    base_ref,
    moved_ref,
    backed_ref,
    neighbor_ref,
    orient_ref,
    normals_ref,
    scale_ref,
    model_ref,
    jump_ref,
    sems,
):
    elements = model_ref.shape[2]
    slots = got_ref.shape[0] * got_ref.shape[1]
    copies = fetch(
        [
            (neighbor_hbm, neighbor_ref),
            (orient_hbm, orient_ref),
            (normals_hbm, normals_ref),
            (scale_hbm, scale_ref),
            (model_hbm, model_ref),
        ],
        sems,
    )
    received = got_ref[...].reshape(slots, got_ref.shape[2])[:, 0:ROWS].T
    high, low = split(received)
    received = jnp.concatenate([high, low], axis=1)
    for copy in copies[0:2]:
        copy.wait()
    for f in range(4):
        lanes = slice(f * elements, (f + 1) * elements)
        picked = one_hot(neighbor_ref[f : f + 1], slots, 4 * elements)
        outer = dot(received, jnp.concatenate([picked, picked], axis=0))
        index = turn_rows(turning, orient_ref[f : f + 1])
        for cs in range(27):
            r = slice(16 * cs, 16 * cs + 16)
            jump_ref[r, lanes] = own_ref[r, lanes] + rotate(outer[r], index)
    for copy in copies[2:]:
        copy.wait()
    lift = lift_ref[...]

    def lifted(pieces):
        high, low = split(jnp.concatenate(pieces, axis=0))
        return dot(lift, jnp.concatenate([high, low, high], axis=0))[0:NODES]

    scaled, normal = [], []
    for f in range(4):
        half = 0.5 * scale_ref[f : f + 1]
        scaled.append(half)
        normal.append([half * normals_ref[j, f : f + 1] for j in range(3)])

    def flux(s):
        def jump(c, f):
            r = (s * 9 + c) * 16
            return jump_ref[r : r + 16, f * elements : (f + 1) * elements]

        result = []
        for i in range(3):
            result.append(
                lifted(
                    [
                        sum(normal[f][j] * jump(3 + stress_of[i][j], f) for j in range(3))
                        for f in range(4)
                    ]
                )
            )
        for i, j in voigt_pairs:
            if i == j:
                result.append(lifted([(2.0 * normal[f][i]) * jump(i, f) for f in range(4)]))
            else:
                result.append(
                    lifted(
                        [
                            normal[f][i] * jump(j, f) + normal[f][j] * jump(i, f)
                            for f in range(4)
                        ]
                    )
                )
        if s == 0:
            return result, None
        return result, [lifted([scaled[f] * jump(c, f) for f in range(4)]) for c in range(9)]

    terms, _ = flux(0)
    for c in range(9):
        base_ref[c] = vol0_ref[c] + terms[c]
    for s, vol_ref, out in ((1, vol1_ref, moved_ref), (2, vol2_ref, backed_ref)):
        terms, pen = flux(s)
        values = model_terms(model_ref[0], model_ref[1], model_ref[2], terms)
        for c in range(9):
            out[c] = vol_ref[c] + time_step * (values[c] + pen[c])


def step_kernel(
    regions,
    *refs,
):
    blocks, refs = refs[:regions], refs[regions:]
    (
        base_ref,
        moved_ref,
        backed_ref,
        prolong_ref,
        restrict_ref,
        observe_hbm,
        owner_hbm,
        local_hbm,
        child_hbm,
        delta_ref,
        adjoint_ref,
        message_ref,
        observe_ref,
        owner_ref,
        local_ref,
        child_ref,
        spread_ref,
        sems,
    ) = refs
    elements = observe_ref.shape[1]
    devices = message_ref.shape[0]
    width = message_ref.shape[2] // 4
    share = blocks[0].shape[1]
    waves = share // width
    copies = fetch(
        [
            (owner_hbm, owner_ref),
            (local_hbm, local_ref),
            (child_hbm, child_ref),
            (observe_hbm, observe_ref),
        ],
        sems,
    )
    for copy in copies:
        copy.wait()
    owner, local = owner_ref[...], local_ref[...]
    away = owner // waves - lax.axis_index("region")
    away = jnp.where(away < 0, away + regions, away)
    place = away * share + lax.rem(owner, waves) * width + local
    total = None
    for s in range(regions):
        high, low = split(blocks[s][...])
        hot = one_hot(place, share, s * share)
        part = dot(jnp.concatenate([high, low], axis=0), hot)
        total = part if total is None else total + part
    fetched = total[0:32] + total[32:64]
    owner_hot = one_hot(owner, devices)
    local_hot = jnp.where(
        lax.broadcasted_iota(jnp.int32, (width, elements), 0) == local, 1.0, 0.0
    )
    child_hot = jnp.where(
        lax.broadcasted_iota(jnp.int32, (8, elements), 0) == child_ref[...], 1.0, 0.0
    )
    prolong = prolong_ref[...]
    step_fine = []
    for p in range(3):
        masked = jnp.concatenate(
            [fetched[10 * p + k : 10 * p + k + 1] * child_hot for k in range(10)], axis=0
        )
        high, low = split(masked)
        step_fine.append(dot(prolong, jnp.concatenate([high, low, high], axis=0))[0:NODES])
    base = [base_ref[c] for c in range(9)]
    pushed = model_terms(step_fine[0], step_fine[1], step_fine[2], base)
    observe = time_step * observe_ref[...]
    ahead = []
    for c in range(9):
        value = moved_ref[c] + time_step * pushed[c]
        delta_ref[c] = value
        value = backed_ref[c] + observe * value
        adjoint_ref[c] = value
        ahead.append(value)
    grads = [
        time_step * sum(ahead[i] * base[i] for i in range(3)),
        (0.5 * time_step) * ((ahead[3] + ahead[4] + ahead[5]) * (base[3] + base[4] + base[5])),
        time_step * sum(ahead[c] * base[c] for c in range(3, 9)),
    ]
    owner_twice = jnp.concatenate([owner_hot, owner_hot], axis=1)
    used = 30 * width
    spread_ref[used:] = jnp.zeros((spread_ref.shape[0] - used, 2 * elements), BF16)
    for p in range(3):
        high, low = split(pad_rows(grads[p], KROW))
        parts = dot(restrict_ref[...], jnp.concatenate([high, low, high], axis=0))
        for k in range(10):
            row = jnp.sum(parts[8 * k : 8 * k + 8] * child_hot, axis=0, keepdims=True)
            high, low = split(row * local_hot)
            at = (10 * p + k) * width
            spread_ref[at : at + width] = jnp.concatenate([high, low], axis=1)
    gathered = dot_nt(owner_twice, spread_ref[...])
    for s in range(message_ref.shape[1]):
        message_ref[:, s, :] = gathered[:, s * 4 * width : (s + 1) * 4 * width]


def sum_kernel(arrived_ref, reg_ref, coarse_ref, out_ref):
    width = coarse_ref.shape[1]
    total = jnp.sum(arrived_ref[...], axis=0)
    weighted = reg_ref[...] * coarse_ref[...]
    for row in range(coarse_ref.shape[0]):
        s, j = row // 4, row % 4
        out_ref[row : row + 1] = (
            total[s : s + 1, j * width : (j + 1) * width] + weighted[row : row + 1]
        )


HBM, VMEM = pltpu.MemorySpace.HBM, pltpu.MemorySpace.VMEM


def call(kernel, name, ins, outs, scratch=(), limit=16 << 20, flops=0, bytes_accessed=0):
    specs = {
        "h": pl.BlockSpec(memory_space=HBM),
        "v": pl.BlockSpec(memory_space=VMEM),
        "w": pl.BlockSpec(),
    }
    shapes = []
    for how, shape, dtype in outs:
        if how == "h":
            shapes.append(HBM(shape, dtype))
        elif how == "v":
            shapes.append(VMEM(shape, dtype))
        else:
            shapes.append(jax.ShapeDtypeStruct(shape, dtype))
    run = pl.pallas_call(
        kernel,
        out_shape=tuple(shapes),
        in_specs=[specs[how] for how in ins],
        out_specs=tuple(specs[how] for how, _, _ in outs),
        scratch_shapes=list(scratch),
        name=name,
        cost_estimate=pl.CostEstimate(
            flops=flops, bytes_accessed=bytes_accessed, transcendentals=0
        ),
        compiler_params=pltpu.CompilerParams(vmem_limit_bytes=limit),
    )

    def placed(*operands):
        fixed = [
            pltpu.with_memory_space_constraint(x, VMEM if how == "v" else HBM)
            for how, x in zip(ins, operands, strict=True)
        ]
        return run(*fixed)

    return placed


def body(
    state0,
    delta,
    adjoint,
    model,
    geometry,
    normals,
    face_scale,
    derivative,
    lift,
    prolong,
    coarse_step,
    reg_weight,
    observe,
    owner,
    coarse_local,
    child,
    neighbor,
    orient,
    send_face,
):
    face_index, turning = tables()
    elements = state0.shape[2]
    wave_size = lax.axis_size("wave")
    devices = lax.axis_size(("region", "wave"))
    sends = send_face.shape[0]
    block, width = coarse_step.shape
    packs = 8
    everyone = ("region", "wave")
    select = np.zeros((64, 2 * KROW), np.float32)
    for f in range(4):
        for m in range(FACE):
            select[16 * f + m, face_index[m, f]] = 1.0
            select[16 * f + m, KROW + face_index[m, f]] = 1.0
    slots = sends // wave_size
    regions = devices // wave_size
    lanes = ROWS + spare(block, slots) * width
    lanes = -(-lanes // 128) * 128
    faces = 4 * elements
    state = (9, NODES, elements)

    high, low, sent = call(
        send_kernel,
        "send",
        "hhhhhh",
        (
            ("h", (ROWS, faces), BF16),
            ("h", (ROWS, faces), BF16),
            ("w", (wave_size, slots, lanes), F32),
        ),
        scratch=(
            pltpu.VMEM((3, 9, NODES, elements), F32),
            pltpu.VMEM(select.shape, BF16),
            pltpu.VMEM((1, sends), jnp.int32),
            pltpu.VMEM((block, width), F32),
            pltpu.VMEM((ROWS, faces), BF16),
            pltpu.VMEM((ROWS, faces), BF16),
            pltpu.SemaphoreType.DMA((6,)),
            pltpu.SemaphoreType.DMA((3, 2)),
        ),
        bytes_accessed=3 << 20,
        flops=1 << 28,
    )(state0, delta, adjoint, jnp.asarray(select, BF16), send_face.reshape(1, sends), coarse_step)
    got = lax.all_to_all(sent, "wave", split_axis=0, concat_axis=0, tiled=True)
    own, vol0, vol1, vol2, lift_left, prolong_left, restrict_left = call(
        functools.partial(own_kernel, turning),
        "own",
        "w" * 12,
        (
            ("v", (ROWS, faces), F32),
            ("v", state, F32),
            ("v", state, F32),
            ("v", state, F32),
            ("v", (VROW, 192), BF16),
            ("v", (VROW, 240), BF16),
            ("v", (80, 3 * KROW), BF16),
        ),
        scratch=(pltpu.VMEM((3 * VROW, 3 * KROW), F32), pltpu.VMEM((128, 128), F32)),
        limit=32 << 20,
        bytes_accessed=8 << 20,
        flops=1 << 32,
    )(
        state0,
        delta,
        adjoint,
        model,
        geometry,
        neighbor,
        orient,
        derivative,
        lift.transpose(2, 0, 1),
        prolong.transpose(2, 0, 1),
        high,
        low,
    )
    rows = spare(block, slots) * slots
    (near,) = call(pick_kernel, "pick", "v", (("v", (rows, wave_size * width), F32),), limit=4 << 20)(got)
    blocks = [near]
    for s in range(1, regions):
        pairs = [(i, (i - s) % regions) for i in range(regions)]
        blocks.append(lax.ppermute(near, "region", pairs))
    base, moved, backed = call(
        functools.partial(jump_kernel, turning),
        "jump",
        "vhh" + "v" + "v" + "hh" + "v" * 3 + "h",
        (("v", state, F32),) * 3,
        scratch=(
            pltpu.VMEM((4, elements), jnp.int32),
            pltpu.VMEM((4, elements), jnp.int32),
            pltpu.VMEM((3, 4, elements), F32),
            pltpu.VMEM((4, elements), F32),
            pltpu.VMEM((3, NODES, elements), F32),
            pltpu.VMEM((ROWS, faces), F32),
            pltpu.SemaphoreType.DMA((5,)),
        ),
        bytes_accessed=8 << 20,
        flops=1 << 31,
    )(got, neighbor, orient, own, lift_left, normals, face_scale, vol0, vol1, vol2, model)
    delta_next, adjoint_next, message = call(
        functools.partial(step_kernel, regions),
        "step",
        "v" * (regions + 3) + "v" + "v" + "h" * 4,
        (("w", state, F32), ("w", state, F32), ("v", (devices, packs, 4 * width), F32)),
        scratch=(
            pltpu.VMEM((NODES, elements), F32),
            pltpu.VMEM((1, elements), jnp.int32),
            pltpu.VMEM((1, elements), jnp.int32),
            pltpu.VMEM((1, elements), jnp.int32),
            pltpu.VMEM((packs * 4 * width, 2 * elements), BF16),
            pltpu.SemaphoreType.DMA((4,)),
        ),
        limit=12 << 20,
        bytes_accessed=4 << 20,
        flops=1 << 30,
    )(
        *blocks,
        base,
        moved,
        backed,
        prolong_left,
        restrict_left,
        observe,
        owner.reshape(1, elements),
        coarse_local.reshape(1, elements),
        child.reshape(1, elements),
    )
    arrived = lax.all_to_all(message, everyone, split_axis=0, concat_axis=0, tiled=True)
    (hess_vec,) = call(
        sum_kernel, "total", "vvv", (("w", (block, width), F32),), limit=4 << 20
    )(arrived, reg_weight, coarse_step)
    return (delta_next, adjoint_next, hess_vec)


def solution(mesh):
    both = ("region", "wave")
    wide, flat = P(None, None, both), P(None, both)
    placed = (
        wide,
        wide,
        wide,
        wide,
        flat,
        wide,
        flat,
        P(),
        P(),
        P(),
        flat,
        flat,
        flat,
        P(both, None),
        P(both),
        P(both),
        flat,
        flat,
        P(both),
    )
    return jax.shard_map(
        body, mesh=mesh, in_specs=placed, out_specs=(wide, wide, flat), check_vma=False
    )
```

```python
import functools
import jax
import jax.numpy as jnp
import numpy as np
from jax import lax
from jax.experimental import pallas as pl
from jax.experimental.pallas import tpu as pltpu
from jax.sharding import PartitionSpec as P

time_step = 0.2
penalty = 0.5
stress_of = ((0, 5, 4), (5, 1, 3), (4, 3, 2))
voigt_pairs = ((0, 0), (1, 1), (2, 2), (1, 2), (0, 2), (0, 1))
F32 = jnp.float32
BF16 = jnp.bfloat16
NODES, FACE, ROWS, BLOCK = 35, 15, 27 * 16, 30
VROW = 40
KROW = 48


def tables():
    triangle = [(one, two) for one in range(5) for two in range(5 - one)]
    volume_nodes = [
        (one, two, three)
        for one in range(5)
        for two in range(5 - one)
        for three in range(5 - one - two)
    ]
    face_index = np.zeros((15, 4), np.int32)
    for entry, (a, b) in enumerate(triangle):
        for face, key in enumerate([(a, b, 0), (a, 0, b), (0, a, b), (a, b, 4 - a - b)]):
            face_index[entry, face] = volume_nodes.index(key)
    orders = [(0, 1, 2), (1, 2, 0), (2, 0, 1), (0, 2, 1), (2, 1, 0), (1, 0, 2)]
    turning = np.zeros((6, 15), np.int32)
    for orient_id, order in enumerate(orders):
        for entry, (a, b) in enumerate(triangle):
            coords = (a, b, 4 - a - b)
            turning[orient_id, entry] = triangle.index((coords[order[0]], coords[order[1]]))
    return face_index, turning


def split(x):
    high = x.astype(BF16)
    low = (x - high.astype(F32)).astype(BF16)
    return high, low


def dot(a, b):
    return jnp.dot(a, b, preferred_element_type=F32)


def dot_nt(a, b):
    return lax.dot_general(a, b, (((1,), (1,)), ((), ())), preferred_element_type=F32)


def pad_rows(x, rows):
    return jnp.concatenate([x, jnp.zeros((rows - x.shape[0],) + x.shape[1:], x.dtype)], axis=0)


def one_hot(ids, count, start=0):
    rows = lax.broadcasted_iota(jnp.int32, (count, ids.shape[1]), 0) + start
    return jnp.where(rows == ids, 1.0, 0.0).astype(BF16)


def turn_rows(turning, orient_row):
    lanes = orient_row.shape[1]
    rows = lax.broadcasted_iota(jnp.int32, (16, lanes), 0)
    result = rows
    for orient_id in range(1, 6):
        table = jnp.zeros((16, lanes), jnp.int32)
        for m in range(15):
            table = jnp.where(rows == m, int(turning[orient_id, m]), table)
        result = jnp.where(orient_row == orient_id, table, result)
    return result


def rotate(x, index):
    first, second = x[0:8], x[8:16]
    halves = []
    for h in range(2):
        part = index[8 * h : 8 * h + 8]
        inside = part & 7
        a = jnp.take_along_axis(first, inside, axis=0)
        b = jnp.take_along_axis(second, inside, axis=0)
        halves.append(jnp.where(part < 8, a, b))
    return jnp.concatenate(halves, axis=0)


def fetch(pairs, sems):
    copies = []
    for index, (source, target) in enumerate(pairs):
        copy = pltpu.make_async_copy(source, target, sems.at[index])
        copy.start()
        copies.append(copy)
    return copies


def gather_kernel(
    q0_hbm,
    q1_hbm,
    q2_hbm,
    select_hbm,
    send_hbm,
    coarse_hbm,
    sent_ref,
    coarse_ref,
    q_ref,
    select_ref,
    send_ref,
    sems,
):
    elements = q_ref.shape[3]
    sends = sent_ref.shape[1]
    copies = fetch(
        [
            (send_hbm, send_ref),
            (q0_hbm, q_ref.at[0]),
            (q1_hbm, q_ref.at[1]),
            (q2_hbm, q_ref.at[2]),
            (select_hbm, select_ref),
            (coarse_hbm, coarse_ref),
        ],
        sems,
    )
    copies[0].wait()
    face = send_ref[...] // elements
    picked = one_hot(send_ref[...] - face * elements, elements)
    twice = jnp.concatenate([face, face], axis=1)

    def pick_elements(s):
        copies[1 + s].wait()
        pieces = []
        for c in range(9):
            pieces += split(pad_rows(q_ref[s, c], KROW))
        return dot(jnp.concatenate(pieces, axis=0), picked).astype(BF16)

    def pick_faces(s, nodes):
        for c in range(0, 9, 2):
            parts = [nodes[2 * KROW * k : 2 * KROW * (k + 1)] for k in range(c, min(c + 2, 9))]
            every = dot(select_ref[...], jnp.concatenate(parts, axis=1))
            which = twice[:, 0 : every.shape[1]]
            value = every[0:16]
            for f in range(1, 4):
                value = jnp.where(which == f, every[16 * f : 16 * f + 16], value)
            for k in range(len(parts)):
                row = (s * 9 + c + k) * 16
                sent_ref[row : row + 16] = value[:, k * sends : (k + 1) * sends]

    nodes = [pick_elements(0), pick_elements(1)]
    copies[4].wait()
    pick_faces(0, nodes[0])
    nodes.append(pick_elements(2))
    pick_faces(1, nodes[1])
    pick_faces(2, nodes[2])
    copies[5].wait()


def pack_kernel(sent_ref, coarse_ref, out_ref):
    waves = out_ref.shape[0]
    slots = sent_ref.shape[1] // waves
    block, width = coarse_ref.shape
    sent = sent_ref[...].T
    for t in range(4):
        part = sent[:, 128 * t : min(128 * t + 128, ROWS)]
        out_ref[:, t * slots : (t + 1) * slots, 0 : part.shape[1]] = part.reshape(
            waves, slots, part.shape[1]
        )
    pieces = spare(block, slots)
    row = 4 * slots
    if fits(block, slots, width):
        own = pad_rows(coarse_ref[...], pieces * slots)
        for h in range(pieces):
            part = own[h * slots : (h + 1) * slots]
            at = ROWS - 384 + h * width
            for w in range(waves):
                out_ref[w, 3 * slots : 4 * slots, at : at + width] = part
    else:
        padded = pad_rows(coarse_ref[...], 32)
        part = jnp.concatenate([padded[8 * j : 8 * j + 8] for j in range(4)], axis=1)
        for w in range(waves):
            out_ref[w, row : row + 8, 0 : 4 * width] = part


def fits(block, slots, width):
    return spare(block, slots) * width <= 512 - ROWS


def spare(block, slots):
    return -(-block // slots)


def pick_kernel(slots, got_ref, out_ref):
    waves = got_ref.shape[0]
    width = out_ref.shape[1] // waves
    for w in range(waves):
        lanes = slice(w * width, (w + 1) * width)
        if fits(BLOCK, slots, width):
            for h in range(spare(BLOCK, slots)):
                at = ROWS - 384 + h * width
                out_ref[h * slots : (h + 1) * slots, lanes] = got_ref[
                    w, 3 * slots : 4 * slots, at : at + width
                ]
        else:
            part = got_ref[w, 4 * slots : 4 * slots + 8]
            for j in range(4):
                out_ref[8 * j : 8 * j + 8, lanes] = part[:, j * width : (j + 1) * width]


def own_kernel(
    turning,
    regions,
    width,
    q0_ref,
    q1_ref,
    q2_ref,
    model_ref,
    geometry_ref,
    neighbor_ref,
    orient_ref,
    derivative_ref,
    lift_ref,
    prolong_ref,
    select_ref,
    normals_ref,
    scale_ref,
    owner_ref,
    local_ref,
    child_ref,
    own_ref,
    vol0_ref,
    vol1_ref,
    vol2_ref,
    lift_out,
    prolong_out,
    restrict_out,
    index_out,
    place_out,
    child_out,
    send_out,
    model_out,
    half_out,
    normal_out,
    left_ref,
    rows_ref,
    trace_ref,
    high_ref,
    low_ref,
):
    elements = q0_ref.shape[2]
    owner = owner_ref[...]
    waves = place_out.shape[0] // (width * regions)
    away = (owner // waves) ^ lax.axis_index("region")
    place = (away * waves + lax.rem(owner, waves)) * width + local_ref[...]
    place_out[...] = one_hot(place, place_out.shape[0])
    devices = place_out.shape[0] // width
    deep = send_out.shape[0] // devices
    column = jnp.broadcast_to(owner.astype(F32), (128, elements)).T
    earlier = []
    for t in range(elements // 128):
        lanes = slice(128 * t, 128 * t + 128)
        rows = lax.broadcasted_iota(jnp.int32, (elements, 128), 0)
        lane = lax.broadcasted_iota(jnp.int32, (elements, 128), 1) + 128 * t
        same = jnp.where(column == owner[:, lanes].astype(F32), 1, 0)
        same = jnp.where(rows < lane, same, 0)
        earlier.append(jnp.sum(same, axis=0, keepdims=True))
    rank = jnp.concatenate(earlier, axis=1)
    group = rank // deep
    spot = owner * deep + (rank - group * deep)
    for q in range(4):
        send_out[:, q * elements : (q + 1) * elements] = one_hot(
            jnp.where(group == q, spot, -1), devices * deep
        )
    child_out[...] = jnp.where(
        lax.broadcasted_iota(jnp.int32, child_out.shape, 0) == child_ref[...], 1.0, 0.0
    )
    model_out[...] = model_ref[...]
    half = 0.5 * scale_ref[...]
    half_out[...] = half
    for j in range(3):
        normal_out[j] = half * normals_ref[j]
    left_ref[...] = jnp.zeros_like(left_ref)
    for k in range(3):
        high, low = split(derivative_ref[k])
        r = k * VROW
        left_ref[r : r + NODES, 0:NODES] = high.astype(F32)
        left_ref[r : r + NODES, KROW : KROW + NODES] = high.astype(F32)
        left_ref[r : r + NODES, 2 * KROW : 2 * KROW + NODES] = low.astype(F32)
    left = jnp.concatenate([left_ref[...].astype(BF16), select_ref[...]], axis=0)
    rows_ref[...] = jnp.zeros_like(rows_ref)
    for f in range(4):
        rows_ref[16 * f : 16 * f + FACE, 0:NODES] = time_step * lift_ref[:, f, :]
    turned = rows_ref[...].T
    high, low = split(turned[0:VROW, 0:64])
    lift_out[...] = jnp.concatenate([high, high, low], axis=1)
    rows_ref[...] = jnp.zeros_like(rows_ref)
    rows_ref[0:80, 0:NODES] = prolong_ref[...].reshape(80, NODES)
    plain = rows_ref[...]
    high, low = split(plain[0:80, 0:KROW])
    restrict_out[...] = jnp.concatenate([high, high, low], axis=1)
    turned = plain.T
    high, low = split(turned[0:VROW, 0:80])
    prolong_out[...] = jnp.concatenate([high, high, low], axis=1)

    geometry = geometry_ref[...]
    for s, (ref, out) in enumerate(
        ((q0_ref, vol0_ref), (q1_ref, vol1_ref), (q2_ref, vol2_ref))
    ):
        local = []
        for c in range(9):
            high, low = split(pad_rows(ref[c], KROW))
            both = dot(left, jnp.concatenate([high, low, high], axis=0))
            local.append(both)
            row = (s * 9 + c) * 16
            for f in range(4):
                at = 3 * VROW + 16 * f
                lanes = slice(f * elements, (f + 1) * elements)
                trace = both[at : at + 16]
                trace_ref[row : row + 16, lanes] = trace
                high_ref[row : row + 16, lanes], low_ref[row : row + 16, lanes] = split(trace)

        def grad(c, i):
            total = None
            for k in range(3):
                term = geometry[3 * i + k : 3 * i + k + 1] * local[c][k * VROW : k * VROW + VROW]
                total = term if total is None else total + term
            return total[0:NODES]

        terms = []
        for i in range(3):
            terms.append(sum(grad(3 + stress_of[i][j], j) for j in range(3)))
        for i, j in voigt_pairs:
            terms.append(2.0 * grad(i, i) if i == j else grad(j, i) + grad(i, j))
        if s == 0:
            for c in range(9):
                out[c] = time_step * terms[c]
        else:
            trace = (0.5 * model_ref[1]) * (terms[3] + terms[4] + terms[5])
            for c in range(9):
                value = (model_ref[0] if c < 3 else model_ref[2]) * terms[c]
                if 3 <= c < 6:
                    value = value + trace
                out[c] = ref[c] + time_step * value

    for f in range(4):
        lanes = slice(f * elements, (f + 1) * elements)
        picked = one_hot(neighbor_ref[f : f + 1], 4 * elements)
        outer = dot(high_ref[...], picked) + dot(low_ref[...], picked)
        index = turn_rows(turning, orient_ref[f : f + 1])
        index_out[:, lanes] = index
        for cs in range(27):
            r = slice(16 * cs, 16 * cs + 16)
            own_ref[r, lanes] = rotate(outer[r], index) - trace_ref[r, lanes]


def model_terms(first, second, third, terms):
    trace = (0.5 * second) * (terms[3] + terms[4] + terms[5])
    values = []
    for c in range(9):
        value = (first if c < 3 else third) * terms[c]
        values.append(value + trace if 3 <= c < 6 else value)
    return values


def turn_kernel(slots, got_ref, index_ref, neighbor_ref, own_ref, jump_ref):
    elements = own_ref.shape[1] // 4
    sends = got_ref.shape[0] * slots
    received = []
    for t in range(4):
        part = got_ref[:, t * slots : (t + 1) * slots, :].reshape(sends, 128).T
        received.append(part if t < 3 else part[0 : ROWS - 384])
    high, low = split(jnp.concatenate(received, axis=0))
    received = jnp.concatenate([high, low], axis=1)
    for f in range(4):
        lanes = slice(f * elements, (f + 1) * elements)
        picked = one_hot(neighbor_ref[f : f + 1], sends, 4 * elements)
        outer = dot(received, jnp.concatenate([picked, picked], axis=0))
        index = index_ref[:, lanes]
        for cs in range(27):
            r = slice(16 * cs, 16 * cs + 16)
            jump_ref[r, lanes] = own_ref[r, lanes] + rotate(outer[r], index)


def flux_kernel(
    jump_ref,
    lift_ref,
    normal_ref,
    half_ref,
    vol0_ref,
    model_ref,
    base_ref,
    moved_ref,
    backed_ref,
):
    elements = model_ref.shape[2]
    lift = lift_ref[...]

    def lifted(pieces):
        high, low = split(jnp.concatenate(pieces, axis=0))
        return dot(lift, jnp.concatenate([high, low, high], axis=0))[0:NODES]

    scaled = [half_ref[f : f + 1] for f in range(4)]
    normal = [[normal_ref[j, f : f + 1] for j in range(3)] for f in range(4)]

    def flux(s):
        def jump(c, f):
            r = (s * 9 + c) * 16
            return jump_ref[r : r + 16, f * elements : (f + 1) * elements]

        result = []
        for i in range(3):
            result.append(
                lifted(
                    [
                        sum(normal[f][j] * jump(3 + stress_of[i][j], f) for j in range(3))
                        for f in range(4)
                    ]
                )
            )
        for i, j in voigt_pairs:
            if i == j:
                result.append(lifted([(2.0 * normal[f][i]) * jump(i, f) for f in range(4)]))
            else:
                result.append(
                    lifted(
                        [
                            normal[f][i] * jump(j, f) + normal[f][j] * jump(i, f)
                            for f in range(4)
                        ]
                    )
                )
        if s == 0:
            return result, None
        return result, [lifted([scaled[f] * jump(c, f) for f in range(4)]) for c in range(9)]

    terms, _ = flux(0)
    for c in range(9):
        base_ref[c] = vol0_ref[c] + terms[c]
    for s, out in ((1, moved_ref), (2, backed_ref)):
        terms, pen = flux(s)
        values = model_terms(model_ref[0], model_ref[1], model_ref[2], terms)
        for c in range(9):
            out[c] = values[c] + pen[c]


def step_kernel(regions, *refs):
    blocks, refs = refs[:regions], refs[regions:]
    (
    base_ref,
    moved_ref,
    backed_ref,
    prolong_ref,
    restrict_ref,
    place_ref,
    child_ref,
    send_ref,
    local_ref,
    observe_ref,
    vol1_ref,
    vol2_ref,
    delta_ref,
    adjoint_ref,
    message_ref,
    spread_ref,
    ) = refs
    devices = message_ref.shape[0]
    share = blocks[0].shape[1]
    elements = child_ref.shape[1]
    total = None
    for s in range(regions):
        high, low = split(blocks[s][...])
        part = dot(
            jnp.concatenate([high, low], axis=0), place_ref[s * share : (s + 1) * share]
        )
        total = part if total is None else total + part
    fetched = total[0:32] + total[32:64]
    child_hot = child_ref[...]
    prolong = prolong_ref[...]
    step_fine = []
    for p in range(3):
        masked = jnp.concatenate(
            [fetched[10 * p + k : 10 * p + k + 1] * child_hot for k in range(10)], axis=0
        )
        high, low = split(masked)
        step_fine.append(dot(prolong, jnp.concatenate([high, low, high], axis=0))[0:NODES])
    base = [base_ref[c] for c in range(9)]
    pushed = model_terms(step_fine[0], step_fine[1], step_fine[2], base)
    observe = time_step * observe_ref[...]
    ahead = []
    for c in range(9):
        value = (vol1_ref[c] + moved_ref[c]) + pushed[c]
        delta_ref[c] = value
        value = (vol2_ref[c] + backed_ref[c]) + observe * value
        adjoint_ref[c] = value
        ahead.append(value)
    grads = [
        sum(ahead[i] * base[i] for i in range(3)),
        0.5 * ((ahead[3] + ahead[4] + ahead[5]) * (base[3] + base[4] + base[5])),
        sum(ahead[c] * base[c] for c in range(3, 9)),
    ]
    rows = []
    for p in range(3):
        high, low = split(pad_rows(grads[p], KROW))
        parts = dot(restrict_ref[...], jnp.concatenate([high, low, high], axis=0))
        for k in range(10):
            rows.append(
                jnp.sum(parts[8 * k : 8 * k + 8] * child_hot, axis=0, keepdims=True)
            )
    rows.append(local_ref[...].astype(F32))
    high, low = split(pad_rows(jnp.concatenate(rows, axis=0), 32))
    spread_ref[...] = jnp.zeros_like(spread_ref)
    for q in range(4):
        lanes = slice(q * elements, (q + 1) * elements)
        spread_ref[0, 32 * q : 32 * q + 32, lanes] = high
        spread_ref[1, 32 * q : 32 * q + 32, lanes] = low
    sends = send_ref[...]
    packed = dot_nt(sends, spread_ref[0]) + dot_nt(sends, spread_ref[1])
    deep = message_ref.shape[1]
    for d in range(devices):
        message_ref[d] = packed[deep * d : deep * d + deep]


def sum_kernel(
    arrived_ref, reg_ref, coarse_ref, delta_ref, adjoint_ref, out_hbm, delta_hbm, adjoint_hbm, out_ref, sems
):
    copies = fetch([(delta_ref, delta_hbm), (adjoint_ref, adjoint_hbm)], sems.at[pl.ds(0, 2)])
    block, width = coarse_ref.shape
    count, deep, _ = arrived_ref.shape
    values = arrived_ref[...].reshape(count * deep, 128)
    lane = lax.broadcasted_iota(jnp.int32, values.shape, 1)
    local = jnp.concatenate(
        [
            jnp.take_along_axis(
                values[r : r + 8], (lane[0:8] & 96) + block, axis=1
            )
            for r in range(0, count * deep, 8)
        ],
        axis=0,
    )
    hot = jnp.where(local == (lane & 31).astype(F32), 1.0, 0.0).astype(BF16)
    high, low = split(values)
    table = lax.dot_general(
        jnp.concatenate([high, low], axis=0),
        jnp.concatenate([hot, hot], axis=0),
        (((0,), (0,)), ((), ())),
        preferred_element_type=F32,
    )
    total = sum(table[32 * q : 32 * q + 32, 32 * q : 32 * q + 32] for q in range(4))
    weighted = reg_ref[...] * coarse_ref[...]
    out_ref[...] = total[0:block, 0:width] + weighted
    copies += fetch([(out_ref, out_hbm)], sems.at[pl.ds(2, 1)])
    for copy in copies:
        copy.wait()


HBM, VMEM = pltpu.MemorySpace.HBM, pltpu.MemorySpace.VMEM


def call(kernel, name, ins, outs, scratch=(), limit=16 << 20, flops=0, bytes_accessed=0):
    specs = {
        "h": pl.BlockSpec(memory_space=HBM),
        "v": pl.BlockSpec(memory_space=VMEM),
        "w": pl.BlockSpec(),
        "x": pl.BlockSpec(),
    }
    shapes = []
    for how, shape, dtype in outs:
        if how in "hx":
            shapes.append(HBM(shape, dtype))
        elif how == "v":
            shapes.append(VMEM(shape, dtype))
        else:
            shapes.append(jax.ShapeDtypeStruct(shape, dtype))
    run = pl.pallas_call(
        kernel,
        out_shape=tuple(shapes),
        in_specs=[specs[how] for how in ins],
        out_specs=tuple(specs[how] for how, _, _ in outs),
        scratch_shapes=list(scratch),
        name=name,
        cost_estimate=pl.CostEstimate(
            flops=flops, bytes_accessed=bytes_accessed, transcendentals=0
        ),
        compiler_params=pltpu.CompilerParams(vmem_limit_bytes=limit),
    )

    def placed(*operands):
        fixed = [
            pltpu.with_memory_space_constraint(x, VMEM if how == "v" else HBM)
            for how, x in zip(ins, operands, strict=True)
        ]
        return run(*fixed)

    return placed


def body(
    state0,
    delta,
    adjoint,
    model,
    geometry,
    normals,
    face_scale,
    derivative,
    lift,
    prolong,
    coarse_step,
    reg_weight,
    observe,
    owner,
    coarse_local,
    child,
    neighbor,
    orient,
    send_face,
):
    face_index, turning = tables()
    elements = state0.shape[2]
    wave_size = lax.axis_size("wave")
    devices = lax.axis_size(("region", "wave"))
    sends = send_face.shape[0]
    block, width = coarse_step.shape
    deep = 2 * elements // devices // 4
    everyone = ("region", "wave")
    select = np.zeros((64, 2 * KROW), np.float32)
    for f in range(4):
        for m in range(FACE):
            select[16 * f + m, face_index[m, f]] = 1.0
            select[16 * f + m, KROW + face_index[m, f]] = 1.0
    slots = sends // wave_size
    regions = devices // wave_size
    rows = 4 * slots + 8 * (1 - fits(block, slots, width))
    faces = 4 * elements
    state = (9, NODES, elements)

    sent, mine = call(
        gather_kernel,
        "gather",
        "hhhhhh",
        (("v", (ROWS, sends), F32), ("v", (block, width), F32)),
        scratch=(
            pltpu.VMEM((3, *state), F32),
            pltpu.VMEM(select.shape, BF16),
            pltpu.VMEM((1, sends), jnp.int32),
            pltpu.SemaphoreType.DMA((6,)),
        ),
        bytes_accessed=2 << 20,
        flops=1 << 28,
    )(
        state0,
        delta,
        adjoint,
        jnp.asarray(select, BF16),
        send_face.reshape(1, sends),
        coarse_step,
    )
    (message,) = call(
        pack_kernel, "pack", "vv", (("w", (wave_size, rows, 128), F32),), limit=4 << 20
    )(sent, mine)
    got = lax.all_to_all(message, "wave", split_axis=0, concat_axis=0, tiled=True)
    own, vol0, vol1, vol2, lift_left, prolong_left, restrict_left, index, place, kind, places, speeds, half, normal = call(
        functools.partial(own_kernel, turning, regions, width),
        "own",
        "w" * 16,
        (
            ("v", (ROWS, faces), F32),
            ("v", state, F32),
            ("x", state, F32),
            ("x", state, F32),
            ("v", (VROW, 192), BF16),
            ("v", (VROW, 240), BF16),
            ("v", (80, 3 * KROW), BF16),
            ("v", (16, faces), jnp.int32),
            ("v", (devices * width, elements), BF16),
            ("v", (8, elements), F32),
            ("v", (devices * deep, 4 * elements), BF16),
            ("v", (3, NODES, elements), F32),
            ("v", (4, elements), F32),
            ("v", (3, 4, elements), F32),
        ),
        scratch=(
            pltpu.VMEM((3 * VROW, 3 * KROW), F32),
            pltpu.VMEM((128, 128), F32),
            pltpu.VMEM((ROWS, faces), F32),
            pltpu.VMEM((ROWS, faces), BF16),
            pltpu.VMEM((ROWS, faces), BF16),
        ),
        limit=32 << 20,
        bytes_accessed=8 << 20,
        flops=1 << 32,
    )(
        state0,
        delta,
        adjoint,
        model,
        geometry,
        neighbor,
        orient,
        derivative,
        lift.transpose(2, 0, 1),
        prolong.transpose(2, 0, 1),
        jnp.asarray(np.pad(select, ((0, 0), (0, KROW))), BF16),
        normals,
        face_scale,
        owner.reshape(1, elements),
        coarse_local.reshape(1, elements),
        child.reshape(1, elements),
    )
    share = wave_size * width
    (near,) = call(
        functools.partial(pick_kernel, slots), "pick", "v", (("v", (32, share), F32),), limit=4 << 20
    )(got)
    blocks = [near] + [None] * (regions - 1)
    for s in reversed(range(1, regions)):
        blocks[s] = lax.ppermute(near, "region", [(i, i ^ s) for i in range(regions)])
    (jump,) = call(
        functools.partial(turn_kernel, slots),
        "turn",
        "vvvv",
        (("v", (ROWS, faces), F32),),
        bytes_accessed=2 << 20,
        flops=1 << 29,
    )(got, index, neighbor, own)
    base, moved, backed = call(
        flux_kernel,
        "flux",
        "vvvvvv",
        (("v", state, F32),) * 3,
        bytes_accessed=4 << 20,
        flops=1 << 30,
    )(jump, lift_left, normal, half, vol0, speeds)
    delta_next, adjoint_next, message = call(
        functools.partial(step_kernel, regions),
        "step",
        "v" * (regions + 12),
        (("v", state, F32), ("v", state, F32), ("v", (devices, deep, 128), F32)),
        scratch=(pltpu.VMEM((2, 128, 4 * elements), BF16),),
        limit=12 << 20,
        bytes_accessed=4 << 20,
        flops=1 << 30,
    )(*blocks, base, moved, backed, prolong_left, restrict_left, place, kind, places, coarse_local.reshape(1, elements), observe, vol1, vol2)
    arrived = lax.all_to_all(message, everyone, split_axis=0, concat_axis=0, tiled=True)
    hess_vec, delta_next, adjoint_next = call(
        sum_kernel,
        "total",
        "vvvvv",
        (("h", (block, width), F32), ("h", state, F32), ("h", state, F32)),
        scratch=(pltpu.VMEM((block, width), F32), pltpu.SemaphoreType.DMA((3,))),
        limit=4 << 20,
    )(arrived, reg_weight, coarse_step, delta_next, adjoint_next)
    return (delta_next, adjoint_next, hess_vec)


def solution(mesh):
    both = ("region", "wave")
    wide, flat = P(None, None, both), P(None, both)
    placed = (
        wide,
        wide,
        wide,
        wide,
        flat,
        wide,
        flat,
        P(),
        P(),
        P(),
        flat,
        flat,
        flat,
        P(both, None),
        P(both),
        P(both),
        flat,
        flat,
        P(both),
    )
    return jax.shard_map(
        body, mesh=mesh, in_specs=placed, out_specs=(wide, wide, flat), check_vma=False
    )
```

```python
import functools
import jax
import jax.numpy as jnp
import numpy as np
from jax import lax
from jax.experimental import pallas as pl
from jax.experimental.pallas import tpu as pltpu
from jax.sharding import PartitionSpec as P


time_step = 0.2
stress_of = ((0, 5, 4), (5, 1, 3), (4, 3, 2))
voigt_pairs = ((0, 0), (1, 1), (2, 2), (1, 2), (0, 2), (0, 1))
F32 = jnp.float32
BF16 = jnp.bfloat16
NODES, FACE, ROWS, BLOCK = 35, 15, 27 * 16, 30
VROW = 40
KROW = 48


def tables():
    triangle = [(one, two) for one in range(5) for two in range(5 - one)]
    volume_nodes = [
        (one, two, three)
        for one in range(5)
        for two in range(5 - one)
        for three in range(5 - one - two)
    ]
    face_index = np.zeros((15, 4), np.int32)
    for entry, (a, b) in enumerate(triangle):
        for face, key in enumerate([(a, b, 0), (a, 0, b), (0, a, b), (a, b, 4 - a - b)]):
            face_index[entry, face] = volume_nodes.index(key)
    orders = [(0, 1, 2), (1, 2, 0), (2, 0, 1), (0, 2, 1), (2, 1, 0), (1, 0, 2)]
    turning = np.zeros((6, 15), np.int32)
    for orient_id, order in enumerate(orders):
        for entry, (a, b) in enumerate(triangle):
            coords = (a, b, 4 - a - b)
            turning[orient_id, entry] = triangle.index((coords[order[0]], coords[order[1]]))
    return face_index, turning


def split(x):
    high = x.astype(BF16)
    low = (x - high.astype(F32)).astype(BF16)
    return high, low


def dot(a, b):
    return jnp.dot(a, b, preferred_element_type=F32)


def dot_nt(a, b):
    return lax.dot_general(a, b, (((1,), (1,)), ((), ())), preferred_element_type=F32)


def pad_rows(x, rows):
    return jnp.concatenate([x, jnp.zeros((rows - x.shape[0],) + x.shape[1:], x.dtype)], axis=0)


def one_hot(ids, count, start=0):
    rows = lax.broadcasted_iota(jnp.int32, (count, ids.shape[1]), 0) + start
    return jnp.where(rows == ids, 1.0, 0.0).astype(BF16)


def turn_rows(turning, orient_row):
    lanes = orient_row.shape[1]
    rows = lax.broadcasted_iota(jnp.int32, (16, lanes), 0)
    result = rows
    for orient_id in range(1, 6):
        table = jnp.zeros((16, lanes), jnp.int32)
        for m in range(15):
            table = jnp.where(rows == m, int(turning[orient_id, m]), table)
        result = jnp.where(orient_row == orient_id, table, result)
    return result


def rotate(x, index):
    first, second = x[0:8], x[8:16]
    halves = []
    for h in range(2):
        part = index[8 * h : 8 * h + 8]
        inside = part & 7
        a = jnp.take_along_axis(first, inside, axis=0)
        b = jnp.take_along_axis(second, inside, axis=0)
        halves.append(jnp.where(part < 8, a, b))
    return jnp.concatenate(halves, axis=0)


def fetch(pairs, sems):
    copies = []
    for index, (source, target) in enumerate(pairs):
        copy = pltpu.make_async_copy(source, target, sems.at[index])
        copy.start()
        copies.append(copy)
    return copies


def gather_kernel(
    face_index,
    q0_hbm,
    q1_hbm,
    q2_hbm,
    send_hbm,
    coarse_hbm,
    out_ref,
    q_ref,
    send_ref,
    coarse_ref,
    sems,
):
    elements = q_ref.shape[3]
    sends = send_ref.shape[1]
    copies = fetch(
        [
            (send_hbm, send_ref),
            (q0_hbm, q_ref.at[0]),
            (q1_hbm, q_ref.at[1]),
            (q2_hbm, q_ref.at[2]),
            (coarse_hbm, coarse_ref),
        ],
        sems,
    )
    copies[0].wait()
    face = send_ref[...] // elements
    picked = one_hot(send_ref[...] - face * elements, elements)
    rows = lax.broadcasted_iota(jnp.int32, (16, sends), 0)
    index = jnp.zeros((16, sends), jnp.int32)
    for f in range(4):
        table = jnp.zeros((16, sends), jnp.int32)
        for m in range(FACE):
            table = jnp.where(rows == m, int(face_index[m, f]), table)
        index = jnp.where(face == f, table, index)
    inside, tile = index & 7, index >> 3
    for copy in copies[1:]:
        copy.wait()
    fields = [pad_rows(q_ref[s, c], VROW) for s in range(3) for c in range(9)]
    high, low = split(pad_rows(jnp.concatenate(fields, axis=0), len(fields) * VROW + 8))
    count = high.shape[0]
    nodes = dot(jnp.concatenate([high, low], axis=0), picked)
    traces = []
    for at in range(0, len(fields) * VROW, VROW):
        both = nodes[at : at + VROW] + nodes[count + at : count + at + VROW]
        for h in range(0, 16, 8):
            value = None
            for t in range(VROW // 8):
                part = jnp.take_along_axis(both[8 * t : 8 * t + 8], inside[h : h + 8], axis=0)
                value = part if t == 0 else jnp.where(tile[h : h + 8] == t, part, value)
            traces.append(value)
    waves = out_ref.shape[0]
    slots = sends // waves
    block, width = coarse_ref.shape
    sent = jnp.concatenate(traces, axis=0).T
    for t in range(4):
        part = sent[:, 128 * t : min(128 * t + 128, ROWS)]
        out_ref[:, t * slots : (t + 1) * slots, 0 : part.shape[1]] = part.reshape(
            waves, slots, part.shape[1]
        )
    pieces = spare(block, slots)
    row = 4 * slots
    if fits(block, slots, width):
        own = pad_rows(coarse_ref[...], pieces * slots)
        for h in range(pieces):
            part = own[h * slots : (h + 1) * slots]
            at = ROWS - 384 + h * width
            for w in range(waves):
                out_ref[w, 3 * slots : 4 * slots, at : at + width] = part
    else:
        padded = pad_rows(coarse_ref[...], 32)
        part = jnp.concatenate([padded[8 * j : 8 * j + 8] for j in range(4)], axis=1)
        for w in range(waves):
            out_ref[w, row : row + 8, 0 : 4 * width] = part


def fits(block, slots, width):
    return spare(block, slots) * width <= 512 - ROWS


def spare(block, slots):
    return -(-block // slots)


def pick_kernel(slots, got_ref, out_ref):
    waves = got_ref.shape[0]
    width = out_ref.shape[1] // waves
    for w in range(waves):
        lanes = slice(w * width, (w + 1) * width)
        if fits(BLOCK, slots, width):
            for h in range(spare(BLOCK, slots)):
                at = ROWS - 384 + h * width
                out_ref[h * slots : (h + 1) * slots, lanes] = got_ref[
                    w, 3 * slots : 4 * slots, at : at + width
                ]
        else:
            part = got_ref[w, 4 * slots : 4 * slots + 8]
            for j in range(4):
                out_ref[8 * j : 8 * j + 8, lanes] = part[:, j * width : (j + 1) * width]


def own_kernel(
    turning,
    regions,
    width,
    q0_ref,
    q1_ref,
    q2_ref,
    model_ref,
    geometry_ref,
    neighbor_ref,
    orient_ref,
    derivative_ref,
    lift_ref,
    prolong_ref,
    select_ref,
    normals_ref,
    scale_ref,
    owner_ref,
    local_ref,
    child_ref,
    own_ref,
    vol0_ref,
    vol1_ref,
    vol2_ref,
    lift_out,
    prolong_out,
    restrict_out,
    index_out,
    place_out,
    child_out,
    send_out,
    model_out,
    half_out,
    normal_out,
    left_ref,
    rows_ref,
    trace_ref,
    high_ref,
    low_ref,
):
    elements = q0_ref.shape[2]
    owner = owner_ref[...]
    waves = place_out.shape[0] // (width * regions)
    away = (owner // waves) ^ lax.axis_index("region")
    place = (away * waves + lax.rem(owner, waves)) * width + local_ref[...]
    place_out[...] = one_hot(place, place_out.shape[0])
    devices = place_out.shape[0] // width
    deep = send_out.shape[0] // devices
    column = jnp.broadcast_to(owner.astype(F32), (128, elements)).T
    earlier = []
    for t in range(elements // 128):
        lanes = slice(128 * t, 128 * t + 128)
        rows = lax.broadcasted_iota(jnp.int32, (elements, 128), 0)
        lane = lax.broadcasted_iota(jnp.int32, (elements, 128), 1) + 128 * t
        same = jnp.where(column == owner[:, lanes].astype(F32), 1, 0)
        same = jnp.where(rows < lane, same, 0)
        earlier.append(jnp.sum(same, axis=0, keepdims=True))
    rank = jnp.concatenate(earlier, axis=1)
    group = rank // deep
    spot = owner * deep + (rank - group * deep)
    for q in range(4):
        send_out[:, q * elements : (q + 1) * elements] = one_hot(
            jnp.where(group == q, spot, -1), devices * deep
        )
    child_out[...] = jnp.where(
        lax.broadcasted_iota(jnp.int32, child_out.shape, 0) == child_ref[...], 1.0, 0.0
    )
    model_out[...] = model_ref[...]
    half = 0.5 * scale_ref[...]
    half_out[...] = half
    for j in range(3):
        normal_out[j] = half * normals_ref[j]
    left_ref[...] = jnp.zeros_like(left_ref)
    for k in range(3):
        high, low = split(derivative_ref[k])
        r = k * VROW
        left_ref[r : r + NODES, 0:NODES] = high.astype(F32)
        left_ref[r : r + NODES, KROW : KROW + NODES] = high.astype(F32)
        left_ref[r : r + NODES, 2 * KROW : 2 * KROW + NODES] = low.astype(F32)
    left = jnp.concatenate([left_ref[...].astype(BF16), select_ref[...]], axis=0)
    rows_ref[...] = jnp.zeros_like(rows_ref)
    for f in range(4):
        rows_ref[16 * f : 16 * f + FACE, 0:NODES] = time_step * lift_ref[:, f, :]
    turned = rows_ref[...].T
    high, low = split(turned[0:VROW, 0:64])
    lift_out[...] = jnp.concatenate([high, high, low], axis=1)
    rows_ref[...] = jnp.zeros_like(rows_ref)
    rows_ref[0:80, 0:NODES] = prolong_ref[...].reshape(80, NODES)
    plain = rows_ref[...]
    high, low = split(plain[0:80, 0:KROW])
    restrict_out[...] = jnp.concatenate([high, high, low], axis=1)
    turned = plain.T
    high, low = split(turned[0:VROW, 0:80])
    prolong_out[...] = jnp.concatenate([high, high, low], axis=1)

    geometry = geometry_ref[...]
    for s, (ref, out) in enumerate(
        ((q0_ref, vol0_ref), (q1_ref, vol1_ref), (q2_ref, vol2_ref))
    ):
        local = []
        for c in range(9):
            high, low = split(pad_rows(ref[c], KROW))
            both = dot(left, jnp.concatenate([high, low, high], axis=0))
            local.append(both)
            row = (s * 9 + c) * 16
            for f in range(4):
                at = 3 * VROW + 16 * f
                lanes = slice(f * elements, (f + 1) * elements)
                trace = both[at : at + 16]
                trace_ref[row : row + 16, lanes] = trace
                high_ref[row : row + 16, lanes], low_ref[row : row + 16, lanes] = split(trace)

        def grad(c, i):
            total = None
            for k in range(3):
                term = geometry[3 * i + k : 3 * i + k + 1] * local[c][k * VROW : k * VROW + VROW]
                total = term if total is None else total + term
            return total[0:NODES]

        terms = []
        for i in range(3):
            terms.append(sum(grad(3 + stress_of[i][j], j) for j in range(3)))
        for i, j in voigt_pairs:
            terms.append(2.0 * grad(i, i) if i == j else grad(j, i) + grad(i, j))
        if s == 0:
            for c in range(9):
                out[c] = time_step * terms[c]
        else:
            trace = (0.5 * model_ref[1]) * (terms[3] + terms[4] + terms[5])
            for c in range(9):
                value = (model_ref[0] if c < 3 else model_ref[2]) * terms[c]
                if 3 <= c < 6:
                    value = value + trace
                out[c] = ref[c] + time_step * value

    for f in range(4):
        lanes = slice(f * elements, (f + 1) * elements)
        picked = one_hot(neighbor_ref[f : f + 1], 4 * elements)
        outer = dot(high_ref[...], picked) + dot(low_ref[...], picked)
        index = turn_rows(turning, orient_ref[f : f + 1])
        index_out[:, lanes] = index
        for cs in range(27):
            r = slice(16 * cs, 16 * cs + 16)
            own_ref[r, lanes] = rotate(outer[r], index) - trace_ref[r, lanes]


def model_terms(first, second, third, terms):
    trace = (0.5 * second) * (terms[3] + terms[4] + terms[5])
    values = []
    for c in range(9):
        value = (first if c < 3 else third) * terms[c]
        values.append(value + trace if 3 <= c < 6 else value)
    return values


def turn_kernel(slots, got_ref, index_ref, neighbor_ref, own_ref, jump_ref):
    elements = own_ref.shape[1] // 4
    sends = got_ref.shape[0] * slots
    received = []
    for t in range(4):
        part = got_ref[:, t * slots : (t + 1) * slots, :].reshape(sends, 128).T
        received.append(part if t < 3 else part[0 : ROWS - 384])
    high, low = split(jnp.concatenate(received, axis=0))
    received = jnp.concatenate([high, low], axis=1)
    for f in range(4):
        lanes = slice(f * elements, (f + 1) * elements)
        picked = one_hot(neighbor_ref[f : f + 1], sends, 4 * elements)
        outer = dot(received, jnp.concatenate([picked, picked], axis=0))
        index = index_ref[:, lanes]
        for cs in range(27):
            r = slice(16 * cs, 16 * cs + 16)
            jump_ref[r, lanes] = own_ref[r, lanes] + rotate(outer[r], index)


def flux_kernel(
    jump_ref,
    lift_ref,
    normal_ref,
    half_ref,
    vol0_ref,
    model_ref,
    base_ref,
    moved_ref,
    backed_ref,
):
    elements = model_ref.shape[2]
    lift = lift_ref[...]

    def lifted(pieces):
        high, low = split(jnp.concatenate(pieces, axis=0))
        return dot(lift, jnp.concatenate([high, low, high], axis=0))[0:NODES]

    scaled = [half_ref[f : f + 1] for f in range(4)]
    normal = [[normal_ref[j, f : f + 1] for j in range(3)] for f in range(4)]

    def flux(s):
        def jump(c, f):
            r = (s * 9 + c) * 16
            return jump_ref[r : r + 16, f * elements : (f + 1) * elements]

        result = []
        for i in range(3):
            result.append(
                lifted(
                    [
                        sum(normal[f][j] * jump(3 + stress_of[i][j], f) for j in range(3))
                        for f in range(4)
                    ]
                )
            )
        for i, j in voigt_pairs:
            if i == j:
                result.append(lifted([(2.0 * normal[f][i]) * jump(i, f) for f in range(4)]))
            else:
                result.append(
                    lifted(
                        [
                            normal[f][i] * jump(j, f) + normal[f][j] * jump(i, f)
                            for f in range(4)
                        ]
                    )
                )
        if s == 0:
            return result, None
        return result, [lifted([scaled[f] * jump(c, f) for f in range(4)]) for c in range(9)]

    terms, _ = flux(0)
    for c in range(9):
        base_ref[c] = vol0_ref[c] + terms[c]
    for s, out in ((1, moved_ref), (2, backed_ref)):
        terms, pen = flux(s)
        values = model_terms(model_ref[0], model_ref[1], model_ref[2], terms)
        for c in range(9):
            out[c] = values[c] + pen[c]


def step_kernel(regions, *refs):
    blocks, refs = refs[:regions], refs[regions:]
    (
    base_ref,
    moved_ref,
    backed_ref,
    prolong_ref,
    restrict_ref,
    place_ref,
    child_ref,
    send_ref,
    local_ref,
    observe_ref,
    vol1_ref,
    vol2_ref,
    delta_ref,
    adjoint_ref,
    message_ref,
    spread_ref,
    ) = refs
    devices = message_ref.shape[0]
    share = blocks[0].shape[1]
    elements = child_ref.shape[1]
    total = None
    for s in range(regions):
        high, low = split(blocks[s][...])
        part = dot(
            jnp.concatenate([high, low], axis=0), place_ref[s * share : (s + 1) * share]
        )
        total = part if total is None else total + part
    fetched = total[0:32] + total[32:64]
    child_hot = child_ref[...]
    prolong = prolong_ref[...]
    step_fine = []
    for p in range(3):
        masked = jnp.concatenate(
            [fetched[10 * p + k : 10 * p + k + 1] * child_hot for k in range(10)], axis=0
        )
        high, low = split(masked)
        step_fine.append(dot(prolong, jnp.concatenate([high, low, high], axis=0))[0:NODES])
    base = [base_ref[c] for c in range(9)]
    pushed = model_terms(step_fine[0], step_fine[1], step_fine[2], base)
    observe = time_step * observe_ref[...]
    ahead = []
    for c in range(9):
        value = (vol1_ref[c] + moved_ref[c]) + pushed[c]
        delta_ref[c] = value
        value = (vol2_ref[c] + backed_ref[c]) + observe * value
        adjoint_ref[c] = value
        ahead.append(value)
    grads = [
        sum(ahead[i] * base[i] for i in range(3)),
        0.5 * ((ahead[3] + ahead[4] + ahead[5]) * (base[3] + base[4] + base[5])),
        sum(ahead[c] * base[c] for c in range(3, 9)),
    ]
    rows = []
    for p in range(3):
        high, low = split(pad_rows(grads[p], KROW))
        parts = dot(restrict_ref[...], jnp.concatenate([high, low, high], axis=0))
        for k in range(10):
            rows.append(
                jnp.sum(parts[8 * k : 8 * k + 8] * child_hot, axis=0, keepdims=True)
            )
    rows.append(local_ref[...].astype(F32))
    high, low = split(pad_rows(jnp.concatenate(rows, axis=0), 32))
    spread_ref[...] = jnp.zeros_like(spread_ref)
    for q in range(4):
        lanes = slice(q * elements, (q + 1) * elements)
        spread_ref[0, 32 * q : 32 * q + 32, lanes] = high
        spread_ref[1, 32 * q : 32 * q + 32, lanes] = low
    sends = send_ref[...]
    packed = dot_nt(sends, spread_ref[0]) + dot_nt(sends, spread_ref[1])
    deep = message_ref.shape[1]
    for d in range(devices):
        message_ref[d] = packed[deep * d : deep * d + deep]


def sum_kernel(
    arrived_ref, reg_ref, coarse_ref, delta_ref, adjoint_ref, out_hbm, delta_hbm, adjoint_hbm, out_ref, sems
):
    copies = fetch([(delta_ref, delta_hbm), (adjoint_ref, adjoint_hbm)], sems.at[pl.ds(0, 2)])
    block, width = coarse_ref.shape
    count, deep, _ = arrived_ref.shape
    values = arrived_ref[...].reshape(count * deep, 128)
    lane = lax.broadcasted_iota(jnp.int32, values.shape, 1)
    local = jnp.concatenate(
        [
            jnp.take_along_axis(
                values[r : r + 8], (lane[0:8] & 96) + block, axis=1
            )
            for r in range(0, count * deep, 8)
        ],
        axis=0,
    )
    hot = jnp.where(local == (lane & 31).astype(F32), 1.0, 0.0).astype(BF16)
    high, low = split(values)
    table = lax.dot_general(
        jnp.concatenate([high, low], axis=0),
        jnp.concatenate([hot, hot], axis=0),
        (((0,), (0,)), ((), ())),
        preferred_element_type=F32,
    )
    total = sum(table[32 * q : 32 * q + 32, 32 * q : 32 * q + 32] for q in range(4))
    weighted = reg_ref[...] * coarse_ref[...]
    out_ref[...] = total[0:block, 0:width] + weighted
    copies += fetch([(out_ref, out_hbm)], sems.at[pl.ds(2, 1)])
    for copy in copies:
        copy.wait()


HBM, VMEM = pltpu.MemorySpace.HBM, pltpu.MemorySpace.VMEM


def call(kernel, ins, outs, scratch=(), limit=16 << 20, flops=0, bytes_accessed=0):
    specs = {
        "h": pl.BlockSpec(memory_space=HBM),
        "v": pl.BlockSpec(memory_space=VMEM),
        "w": pl.BlockSpec(),
        "x": pl.BlockSpec(),
    }
    shapes = []
    for how, shape, dtype in outs:
        if how in "hx":
            shapes.append(HBM(shape, dtype))
        elif how == "v":
            shapes.append(VMEM(shape, dtype))
        else:
            shapes.append(jax.ShapeDtypeStruct(shape, dtype))
    run = pl.pallas_call(
        kernel,
        out_shape=tuple(shapes),
        in_specs=[specs[how] for how in ins],
        out_specs=tuple(specs[how] for how, _, _ in outs),
        scratch_shapes=list(scratch),
        cost_estimate=pl.CostEstimate(
            flops=flops, bytes_accessed=bytes_accessed, transcendentals=0
        ),
        compiler_params=pltpu.CompilerParams(vmem_limit_bytes=limit),
    )

    def placed(*operands):
        fixed = [
            pltpu.with_memory_space_constraint(x, VMEM if how == "v" else HBM)
            for how, x in zip(ins, operands, strict=True)
        ]
        return run(*fixed)

    return placed


def body(
    state0,
    delta,
    adjoint,
    model,
    geometry,
    normals,
    face_scale,
    derivative,
    lift,
    prolong,
    coarse_step,
    reg_weight,
    observe,
    owner,
    coarse_local,
    child,
    neighbor,
    orient,
    send_face,
):
    face_index, turning = tables()
    elements = state0.shape[2]
    wave_size = lax.axis_size("wave")
    devices = lax.axis_size(("region", "wave"))
    sends = send_face.shape[0]
    block, width = coarse_step.shape
    deep = 2 * elements // devices // 4
    everyone = ("region", "wave")
    select = np.zeros((64, 2 * KROW), np.float32)
    for f in range(4):
        for m in range(FACE):
            select[16 * f + m, face_index[m, f]] = 1.0
            select[16 * f + m, KROW + face_index[m, f]] = 1.0
    slots = sends // wave_size
    regions = devices // wave_size
    rows = 4 * slots + 8 * (1 - fits(block, slots, width))
    faces = 4 * elements
    state = (9, NODES, elements)

    (message,) = call(
        functools.partial(gather_kernel, face_index),
        "hhhhh",
        (("w", (wave_size, rows, 128), F32),),
        scratch=(
            pltpu.VMEM((3, *state), F32),
            pltpu.VMEM((1, sends), jnp.int32),
            pltpu.VMEM((block, width), F32),
            pltpu.SemaphoreType.DMA((5,)),
        ),
        bytes_accessed=2 << 20,
        flops=1 << 28,
    )(state0, delta, adjoint, send_face.reshape(1, sends), coarse_step)
    got = lax.all_to_all(message, "wave", split_axis=0, concat_axis=0, tiled=True)
    own, vol0, vol1, vol2, lift_left, prolong_left, restrict_left, index, place, kind, places, speeds, half, normal = call(
        functools.partial(own_kernel, turning, regions, width),
        "w" * 16,
        (
            ("v", (ROWS, faces), F32),
            ("v", state, F32),
            ("x", state, F32),
            ("x", state, F32),
            ("v", (VROW, 192), BF16),
            ("v", (VROW, 240), BF16),
            ("v", (80, 3 * KROW), BF16),
            ("v", (16, faces), jnp.int32),
            ("v", (devices * width, elements), BF16),
            ("v", (8, elements), F32),
            ("v", (devices * deep, 4 * elements), BF16),
            ("v", (3, NODES, elements), F32),
            ("v", (4, elements), F32),
            ("v", (3, 4, elements), F32),
        ),
        scratch=(
            pltpu.VMEM((3 * VROW, 3 * KROW), F32),
            pltpu.VMEM((128, 128), F32),
            pltpu.VMEM((ROWS, faces), F32),
            pltpu.VMEM((ROWS, faces), BF16),
            pltpu.VMEM((ROWS, faces), BF16),
        ),
        limit=32 << 20,
        bytes_accessed=8 << 20,
        flops=1 << 32,
    )(
        state0,
        delta,
        adjoint,
        model,
        geometry,
        neighbor,
        orient,
        derivative,
        lift.transpose(2, 0, 1),
        prolong.transpose(2, 0, 1),
        jnp.asarray(np.pad(select, ((0, 0), (0, KROW))), BF16),
        normals,
        face_scale,
        owner.reshape(1, elements),
        coarse_local.reshape(1, elements),
        child.reshape(1, elements),
    )
    share = wave_size * width
    (near,) = call(
        functools.partial(pick_kernel, slots), "v", (("v", (32, share), F32),), limit=4 << 20
    )(got)
    blocks = [near] + [None] * (regions - 1)
    for s in reversed(range(1, regions)):
        blocks[s] = lax.ppermute(near, "region", [(i, i ^ s) for i in range(regions)])
    (jump,) = call(
        functools.partial(turn_kernel, slots),
        "vvvv",
        (("v", (ROWS, faces), F32),),
        bytes_accessed=2 << 20,
        flops=1 << 29,
    )(got, index, neighbor, own)
    base, moved, backed = call(
        flux_kernel, "vvvvvv", (("v", state, F32),) * 3, bytes_accessed=4 << 20, flops=1 << 30
    )(jump, lift_left, normal, half, vol0, speeds)
    delta_next, adjoint_next, message = call(
        functools.partial(step_kernel, regions),
        "v" * (regions + 12),
        (("v", state, F32), ("v", state, F32), ("v", (devices, deep, 128), F32)),
        scratch=(pltpu.VMEM((2, 128, 4 * elements), BF16),),
        limit=12 << 20,
        bytes_accessed=4 << 20,
        flops=1 << 30,
    )(*blocks, base, moved, backed, prolong_left, restrict_left, place, kind, places, coarse_local.reshape(1, elements), observe, vol1, vol2)
    arrived = lax.all_to_all(message, everyone, split_axis=0, concat_axis=0, tiled=True)
    hess_vec, delta_next, adjoint_next = call(
        sum_kernel,
        "vvvvv",
        (("h", (block, width), F32), ("h", state, F32), ("h", state, F32)),
        scratch=(pltpu.VMEM((block, width), F32), pltpu.SemaphoreType.DMA((3,))),
        limit=4 << 20,
    )(arrived, reg_weight, coarse_step, delta_next, adjoint_next)
    return (delta_next, adjoint_next, hess_vec)


def solution(mesh):
    both = ("region", "wave")
    wide, flat = P(None, None, both), P(None, both)
    placed = (
        wide,
        wide,
        wide,
        wide,
        flat,
        wide,
        flat,
        P(),
        P(),
        P(),
        flat,
        flat,
        flat,
        P(both, None),
        P(both),
        P(both),
        flat,
        flat,
        P(both),
    )
    return jax.shard_map(
        body, mesh=mesh, in_specs=placed, out_specs=(wide, wide, flat), check_vma=False
    )
```

```python
import functools
import jax
import jax.numpy as jnp
import numpy as np
from jax import lax
from jax.experimental import pallas as pl
from jax.experimental.pallas import tpu as pltpu
from jax.sharding import PartitionSpec as P


time_step = 0.2
stress_of = ((0, 5, 4), (5, 1, 3), (4, 3, 2))
voigt_pairs = ((0, 0), (1, 1), (2, 2), (1, 2), (0, 2), (0, 1))
F32 = jnp.float32
BF16 = jnp.bfloat16
NODES, FACE, ROWS, BLOCK = 35, 15, 27 * 16, 30
VROW = 40
KROW = 48


def tables():
    triangle = [(one, two) for one in range(5) for two in range(5 - one)]
    volume_nodes = [
        (one, two, three)
        for one in range(5)
        for two in range(5 - one)
        for three in range(5 - one - two)
    ]
    face_index = np.zeros((15, 4), np.int32)
    for entry, (a, b) in enumerate(triangle):
        for face, key in enumerate([(a, b, 0), (a, 0, b), (0, a, b), (a, b, 4 - a - b)]):
            face_index[entry, face] = volume_nodes.index(key)
    orders = [(0, 1, 2), (1, 2, 0), (2, 0, 1), (0, 2, 1), (2, 1, 0), (1, 0, 2)]
    turning = np.zeros((6, 15), np.int32)
    for orient_id, order in enumerate(orders):
        for entry, (a, b) in enumerate(triangle):
            coords = (a, b, 4 - a - b)
            turning[orient_id, entry] = triangle.index((coords[order[0]], coords[order[1]]))
    return face_index, turning


def split(x):
    high = x.astype(BF16)
    low = (x - high.astype(F32)).astype(BF16)
    return high, low


def dot(a, b):
    return jnp.dot(a, b, preferred_element_type=F32)


def dot_nt(a, b):
    return lax.dot_general(a, b, (((1,), (1,)), ((), ())), preferred_element_type=F32)


def pad_rows(x, rows):
    return jnp.concatenate([x, jnp.zeros((rows - x.shape[0],) + x.shape[1:], x.dtype)], axis=0)


def one_hot(ids, count, start=0):
    rows = lax.broadcasted_iota(jnp.int32, (count, ids.shape[1]), 0) + start
    return jnp.where(rows == ids, 1.0, 0.0).astype(BF16)


def turn_rows(turning, orient_row):
    lanes = orient_row.shape[1]
    rows = lax.broadcasted_iota(jnp.int32, (16, lanes), 0)
    result = rows
    for orient_id in range(1, 6):
        table = jnp.zeros((16, lanes), jnp.int32)
        for m in range(15):
            table = jnp.where(rows == m, int(turning[orient_id, m]), table)
        result = jnp.where(orient_row == orient_id, table, result)
    return result


def rotate(x, index):
    first, second = x[0:8], x[8:16]
    halves = []
    for h in range(2):
        part = index[8 * h : 8 * h + 8]
        inside = part & 7
        a = jnp.take_along_axis(first, inside, axis=0)
        b = jnp.take_along_axis(second, inside, axis=0)
        halves.append(jnp.where(part < 8, a, b))
    return jnp.concatenate(halves, axis=0)


def fetch(pairs, sems):
    copies = []
    for index, (source, target) in enumerate(pairs):
        copy = pltpu.make_async_copy(source, target, sems.at[index])
        copy.start()
        copies.append(copy)
    return copies


def gather_kernel(
    face_index,
    q0_hbm,
    q1_hbm,
    q2_hbm,
    send_hbm,
    coarse_hbm,
    out_ref,
    q_ref,
    send_ref,
    coarse_ref,
    sems,
):
    elements = q_ref.shape[3]
    sends = send_ref.shape[1]
    copies = fetch(
        [
            (q0_hbm, q_ref.at[0]),
            (q1_hbm, q_ref.at[1]),
            (q2_hbm, q_ref.at[2]),
            (send_hbm, send_ref),
            (coarse_hbm, coarse_ref),
        ],
        sems,
    )
    copies[3].wait()
    face = send_ref[...] // elements
    picked = one_hot(send_ref[...] - face * elements, elements)
    rows = lax.broadcasted_iota(jnp.int32, (16, sends), 0)
    index = jnp.zeros((16, sends), jnp.int32)
    for f in range(4):
        table = jnp.zeros((16, sends), jnp.int32)
        for m in range(FACE):
            table = jnp.where(rows == m, int(face_index[m, f]), table)
        index = jnp.where(face == f, table, index)
    inside, tile = index & 7, index >> 3
    for copy in copies[:3] + copies[4:]:
        copy.wait()
    fields = [pad_rows(q_ref[s, c], VROW) for s in range(3) for c in range(9)]
    high, low = split(pad_rows(jnp.concatenate(fields, axis=0), len(fields) * VROW + 8))
    count = high.shape[0]
    nodes = dot(jnp.concatenate([high, low], axis=0), picked)
    traces = []
    for at in range(0, len(fields) * VROW, VROW):
        both = nodes[at : at + VROW] + nodes[count + at : count + at + VROW]
        for h in range(0, 16, 8):
            value = None
            for t in range(VROW // 8):
                part = jnp.take_along_axis(both[8 * t : 8 * t + 8], inside[h : h + 8], axis=0)
                value = part if t == 0 else jnp.where(tile[h : h + 8] == t, part, value)
            traces.append(value)
    waves = out_ref.shape[0]
    slots = sends // waves
    block, width = coarse_ref.shape
    sent = jnp.concatenate(traces, axis=0).T
    for t in range(4):
        part = sent[:, 128 * t : min(128 * t + 128, ROWS)]
        out_ref[:, t * slots : (t + 1) * slots, 0 : part.shape[1]] = part.reshape(
            waves, slots, part.shape[1]
        )
    pieces = spare(block, slots)
    row = 4 * slots
    if fits(block, slots, width):
        own = pad_rows(coarse_ref[...], pieces * slots)
        for h in range(pieces):
            part = own[h * slots : (h + 1) * slots]
            at = ROWS - 384 + h * width
            for w in range(waves):
                out_ref[w, 3 * slots : 4 * slots, at : at + width] = part
    else:
        padded = pad_rows(coarse_ref[...], 32)
        part = jnp.concatenate([padded[8 * j : 8 * j + 8] for j in range(4)], axis=1)
        for w in range(waves):
            out_ref[w, row : row + 8, 0 : 4 * width] = part


def fits(block, slots, width):
    return spare(block, slots) * width <= 512 - ROWS


def spare(block, slots):
    return -(-block // slots)


def pick_kernel(slots, got_ref, out_ref):
    waves = got_ref.shape[0]
    width = out_ref.shape[1] // waves
    for w in range(waves):
        lanes = slice(w * width, (w + 1) * width)
        if fits(BLOCK, slots, width):
            for h in range(spare(BLOCK, slots)):
                at = ROWS - 384 + h * width
                out_ref[h * slots : (h + 1) * slots, lanes] = got_ref[
                    w, 3 * slots : 4 * slots, at : at + width
                ]
        else:
            part = got_ref[w, 4 * slots : 4 * slots + 8]
            for j in range(4):
                out_ref[8 * j : 8 * j + 8, lanes] = part[:, j * width : (j + 1) * width]


def own_kernel(
    turning,
    regions,
    width,
    q0_ref,
    q1_ref,
    q2_ref,
    model_ref,
    geometry_ref,
    neighbor_ref,
    orient_ref,
    derivative_ref,
    lift_ref,
    prolong_ref,
    select_ref,
    normals_ref,
    scale_ref,
    owner_ref,
    local_ref,
    child_ref,
    own_ref,
    vol0_ref,
    vol1_ref,
    vol2_ref,
    lift_out,
    prolong_out,
    restrict_out,
    index_out,
    place_out,
    child_out,
    send_out,
    model_out,
    half_out,
    normal_out,
    left_ref,
    rows_ref,
    trace_ref,
    high_ref,
    low_ref,
):
    elements = q0_ref.shape[2]
    owner = owner_ref[...]
    waves = place_out.shape[0] // (width * regions)
    away = (owner // waves) ^ lax.axis_index("region")
    place = (away * waves + lax.rem(owner, waves)) * width + local_ref[...]
    place_out[...] = one_hot(place, place_out.shape[0])
    devices = place_out.shape[0] // width
    deep = send_out.shape[0] // devices
    column = jnp.broadcast_to(owner.astype(F32), (128, elements)).T
    earlier = []
    for t in range(elements // 128):
        lanes = slice(128 * t, 128 * t + 128)
        rows = lax.broadcasted_iota(jnp.int32, (elements, 128), 0)
        lane = lax.broadcasted_iota(jnp.int32, (elements, 128), 1) + 128 * t
        same = jnp.where(column == owner[:, lanes].astype(F32), 1, 0)
        same = jnp.where(rows < lane, same, 0)
        earlier.append(jnp.sum(same, axis=0, keepdims=True))
    rank = jnp.concatenate(earlier, axis=1)
    group = rank // deep
    spot = owner * deep + (rank - group * deep)
    for q in range(4):
        send_out[:, q * elements : (q + 1) * elements] = one_hot(
            jnp.where(group == q, spot, -1), devices * deep
        )
    child_out[...] = jnp.where(
        lax.broadcasted_iota(jnp.int32, child_out.shape, 0) == child_ref[...], 1.0, 0.0
    )
    model_out[...] = model_ref[...]
    half = 0.5 * scale_ref[...]
    half_out[...] = half
    for j in range(3):
        normal_out[j] = half * normals_ref[j]
    left_ref[...] = jnp.zeros_like(left_ref)
    for k in range(3):
        high, low = split(derivative_ref[k])
        r = k * VROW
        left_ref[r : r + NODES, 0:NODES] = high.astype(F32)
        left_ref[r : r + NODES, KROW : KROW + NODES] = high.astype(F32)
        left_ref[r : r + NODES, 2 * KROW : 2 * KROW + NODES] = low.astype(F32)
    left = jnp.concatenate([left_ref[...].astype(BF16), select_ref[...]], axis=0)
    rows_ref[...] = jnp.zeros_like(rows_ref)
    for f in range(4):
        rows_ref[16 * f : 16 * f + FACE, 0:NODES] = time_step * lift_ref[:, f, :]
    turned = rows_ref[...].T
    high, low = split(turned[0:VROW, 0:64])
    lift_out[...] = jnp.concatenate([high, high, low], axis=1)
    rows_ref[...] = jnp.zeros_like(rows_ref)
    rows_ref[0:80, 0:NODES] = prolong_ref[...].reshape(80, NODES)
    plain = rows_ref[...]
    high, low = split(plain[0:80, 0:KROW])
    restrict_out[...] = jnp.concatenate([high, high, low], axis=1)
    turned = plain.T
    high, low = split(turned[0:VROW, 0:80])
    prolong_out[...] = jnp.concatenate([high, high, low], axis=1)

    geometry = geometry_ref[...]
    for s, (ref, out) in enumerate(
        ((q0_ref, vol0_ref), (q1_ref, vol1_ref), (q2_ref, vol2_ref))
    ):
        local = []
        for c in range(9):
            high, low = split(pad_rows(ref[c], KROW))
            both = dot(left, jnp.concatenate([high, low, high], axis=0))
            local.append(both)
            row = (s * 9 + c) * 16
            for f in range(4):
                at = 3 * VROW + 16 * f
                lanes = slice(f * elements, (f + 1) * elements)
                trace = both[at : at + 16]
                trace_ref[row : row + 16, lanes] = trace
                high_ref[row : row + 16, lanes], low_ref[row : row + 16, lanes] = split(trace)

        def grad(c, i):
            total = None
            for k in range(3):
                term = geometry[3 * i + k : 3 * i + k + 1] * local[c][k * VROW : k * VROW + VROW]
                total = term if total is None else total + term
            return total[0:NODES]

        terms = []
        for i in range(3):
            terms.append(sum(grad(3 + stress_of[i][j], j) for j in range(3)))
        for i, j in voigt_pairs:
            terms.append(2.0 * grad(i, i) if i == j else grad(j, i) + grad(i, j))
        if s == 0:
            for c in range(9):
                out[c] = time_step * terms[c]
        else:
            trace = (0.5 * model_ref[1]) * (terms[3] + terms[4] + terms[5])
            for c in range(9):
                value = (model_ref[0] if c < 3 else model_ref[2]) * terms[c]
                if 3 <= c < 6:
                    value = value + trace
                out[c] = ref[c] + time_step * value

    for f in range(4):
        lanes = slice(f * elements, (f + 1) * elements)
        picked = one_hot(neighbor_ref[f : f + 1], 4 * elements)
        outer = dot(high_ref[...], picked) + dot(low_ref[...], picked)
        index = turn_rows(turning, orient_ref[f : f + 1])
        index_out[:, lanes] = index
        for cs in range(27):
            r = slice(16 * cs, 16 * cs + 16)
            own_ref[r, lanes] = rotate(outer[r], index) - trace_ref[r, lanes]


def model_terms(first, second, third, terms):
    trace = (0.5 * second) * (terms[3] + terms[4] + terms[5])
    values = []
    for c in range(9):
        value = (first if c < 3 else third) * terms[c]
        values.append(value + trace if 3 <= c < 6 else value)
    return values


def turn_kernel(slots, got_ref, index_ref, neighbor_ref, own_ref, jump_ref):
    elements = own_ref.shape[1] // 4
    sends = got_ref.shape[0] * slots
    received = []
    for t in range(4):
        part = got_ref[:, t * slots : (t + 1) * slots, :].reshape(sends, 128).T
        received.append(part if t < 3 else part[0 : ROWS - 384])
    high, low = split(jnp.concatenate(received, axis=0))
    received = jnp.concatenate([high, low], axis=1)
    for f in range(4):
        lanes = slice(f * elements, (f + 1) * elements)
        picked = one_hot(neighbor_ref[f : f + 1], sends, 4 * elements)
        outer = dot(received, jnp.concatenate([picked, picked], axis=0))
        index = index_ref[:, lanes]
        for cs in range(27):
            r = slice(16 * cs, 16 * cs + 16)
            jump_ref[r, lanes] = own_ref[r, lanes] + rotate(outer[r], index)


def flux_kernel(
    jump_ref,
    lift_ref,
    normal_ref,
    half_ref,
    vol0_ref,
    model_ref,
    base_ref,
    moved_ref,
    backed_ref,
):
    elements = model_ref.shape[2]
    lift = lift_ref[...]

    def lifted(pieces):
        high, low = split(jnp.concatenate(pieces, axis=0))
        return dot(lift, jnp.concatenate([high, low, high], axis=0))[0:NODES]

    scaled = [half_ref[f : f + 1] for f in range(4)]
    normal = [[normal_ref[j, f : f + 1] for j in range(3)] for f in range(4)]

    def flux(s):
        def jump(c, f):
            r = (s * 9 + c) * 16
            return jump_ref[r : r + 16, f * elements : (f + 1) * elements]

        result = []
        for i in range(3):
            result.append(
                lifted(
                    [
                        sum(normal[f][j] * jump(3 + stress_of[i][j], f) for j in range(3))
                        for f in range(4)
                    ]
                )
            )
        for i, j in voigt_pairs:
            if i == j:
                result.append(lifted([(2.0 * normal[f][i]) * jump(i, f) for f in range(4)]))
            else:
                result.append(
                    lifted(
                        [
                            normal[f][i] * jump(j, f) + normal[f][j] * jump(i, f)
                            for f in range(4)
                        ]
                    )
                )
        if s == 0:
            return result, None
        return result, [lifted([scaled[f] * jump(c, f) for f in range(4)]) for c in range(9)]

    terms, _ = flux(0)
    for c in range(9):
        base_ref[c] = vol0_ref[c] + terms[c]
    for s, out in ((1, moved_ref), (2, backed_ref)):
        terms, pen = flux(s)
        values = model_terms(model_ref[0], model_ref[1], model_ref[2], terms)
        for c in range(9):
            out[c] = values[c] + pen[c]


def ready_kernel(
    moved_ref, backed_ref, observe_ref, vol1_ref, vol2_ref, delta_ref, adjoint_ref, observe_out
):
    observe = time_step * observe_ref[...]
    observe_out[...] = observe
    for c in range(9):
        value = vol1_ref[c] + moved_ref[c]
        delta_ref[c] = value
        adjoint_ref[c] = (vol2_ref[c] + backed_ref[c]) + observe * value


def step_kernel(regions, *refs):
    blocks, refs = refs[:regions], refs[regions:]
    (
    base_ref,
    moved_ref,
    backed_ref,
    prolong_ref,
    restrict_ref,
    place_ref,
    child_ref,
    send_ref,
    local_ref,
    observe_ref,
    delta_ref,
    adjoint_ref,
    message_ref,
    spread_ref,
    ) = refs
    devices = message_ref.shape[0]
    elements = child_ref.shape[1]
    high, low = split(jnp.concatenate([block[...] for block in blocks], axis=1))
    total = dot(jnp.concatenate([high, low], axis=0), place_ref[...])
    fetched = total[0:32] + total[32:64]
    child_hot = child_ref[...]
    prolong = prolong_ref[...]
    step_fine = []
    for p in range(3):
        masked = jnp.concatenate(
            [fetched[10 * p + k : 10 * p + k + 1] * child_hot for k in range(10)], axis=0
        )
        high, low = split(masked)
        step_fine.append(dot(prolong, jnp.concatenate([high, low, high], axis=0))[0:NODES])
    base = [base_ref[c] for c in range(9)]
    pushed = model_terms(step_fine[0], step_fine[1], step_fine[2], base)
    observe = observe_ref[...]
    ahead = []
    for c in range(9):
        value = moved_ref[c] + pushed[c]
        delta_ref[c] = value
        value = backed_ref[c] + observe * pushed[c]
        adjoint_ref[c] = value
        ahead.append(value)
    grads = [
        sum(ahead[i] * base[i] for i in range(3)),
        0.5 * ((ahead[3] + ahead[4] + ahead[5]) * (base[3] + base[4] + base[5])),
        sum(ahead[c] * base[c] for c in range(3, 9)),
    ]
    rows = []
    for p in range(3):
        high, low = split(pad_rows(grads[p], KROW))
        parts = dot(restrict_ref[...], jnp.concatenate([high, low, high], axis=0))
        for k in range(10):
            rows.append(
                jnp.sum(parts[8 * k : 8 * k + 8] * child_hot, axis=0, keepdims=True)
            )
    rows.append(local_ref[...].astype(F32))
    high, low = split(pad_rows(jnp.concatenate(rows, axis=0), 32))
    spread_ref[...] = jnp.zeros_like(spread_ref)
    for q in range(4):
        lanes = slice(q * elements, (q + 1) * elements)
        spread_ref[0, 32 * q : 32 * q + 32, lanes] = high
        spread_ref[1, 32 * q : 32 * q + 32, lanes] = low
    sends = send_ref[...]
    packed = dot_nt(sends, spread_ref[0]) + dot_nt(sends, spread_ref[1])
    deep = message_ref.shape[1]
    for d in range(devices):
        message_ref[d] = packed[deep * d : deep * d + deep]


def sum_kernel(
    arrived_ref, reg_ref, coarse_ref, delta_ref, adjoint_ref, out_hbm, delta_hbm, adjoint_hbm, out_ref, sems
):
    copies = fetch([(delta_ref, delta_hbm), (adjoint_ref, adjoint_hbm)], sems.at[pl.ds(0, 2)])
    block, width = coarse_ref.shape
    count, deep, _ = arrived_ref.shape
    values = arrived_ref[...].reshape(count * deep, 128)
    lane = lax.broadcasted_iota(jnp.int32, values.shape, 1)
    local = jnp.concatenate(
        [
            jnp.take_along_axis(
                values[r : r + 8], (lane[0:8] & 96) + block, axis=1
            )
            for r in range(0, count * deep, 8)
        ],
        axis=0,
    )
    hot = jnp.where(local == (lane & 31).astype(F32), 1.0, 0.0).astype(BF16)
    high, low = split(values)
    table = lax.dot_general(
        jnp.concatenate([high, low], axis=0),
        jnp.concatenate([hot, hot], axis=0),
        (((0,), (0,)), ((), ())),
        preferred_element_type=F32,
    )
    total = sum(table[32 * q : 32 * q + 32, 32 * q : 32 * q + 32] for q in range(4))
    weighted = reg_ref[...] * coarse_ref[...]
    out_ref[...] = total[0:block, 0:width] + weighted
    copies += fetch([(out_ref, out_hbm)], sems.at[pl.ds(2, 1)])
    for copy in copies:
        copy.wait()


HBM, VMEM = pltpu.MemorySpace.HBM, pltpu.MemorySpace.VMEM


def call(kernel, ins, outs, scratch=(), limit=16 << 20, flops=0, bytes_accessed=0):
    specs = {
        "h": pl.BlockSpec(memory_space=HBM),
        "v": pl.BlockSpec(memory_space=VMEM),
        "w": pl.BlockSpec(),
        "x": pl.BlockSpec(),
    }
    shapes = []
    for how, shape, dtype in outs:
        if how in "hx":
            shapes.append(HBM(shape, dtype))
        elif how == "v":
            shapes.append(VMEM(shape, dtype))
        else:
            shapes.append(jax.ShapeDtypeStruct(shape, dtype))
    run = pl.pallas_call(
        kernel,
        out_shape=tuple(shapes),
        in_specs=[specs[how] for how in ins],
        out_specs=tuple(specs[how] for how, _, _ in outs),
        scratch_shapes=list(scratch),
        cost_estimate=pl.CostEstimate(
            flops=flops, bytes_accessed=bytes_accessed, transcendentals=0
        ),
        compiler_params=pltpu.CompilerParams(vmem_limit_bytes=limit),
    )

    def placed(*operands):
        fixed = [
            pltpu.with_memory_space_constraint(x, VMEM if how == "v" else HBM)
            for how, x in zip(ins, operands, strict=True)
        ]
        return run(*fixed)

    return placed


def body(
    state0,
    delta,
    adjoint,
    model,
    geometry,
    normals,
    face_scale,
    derivative,
    lift,
    prolong,
    coarse_step,
    reg_weight,
    observe,
    owner,
    coarse_local,
    child,
    neighbor,
    orient,
    send_face,
):
    face_index, turning = tables()
    elements = state0.shape[2]
    wave_size = lax.axis_size("wave")
    devices = lax.axis_size(("region", "wave"))
    sends = send_face.shape[0]
    block, width = coarse_step.shape
    deep = 2 * elements // devices // 4
    everyone = ("region", "wave")
    select = np.zeros((64, 2 * KROW), np.float32)
    for f in range(4):
        for m in range(FACE):
            select[16 * f + m, face_index[m, f]] = 1.0
            select[16 * f + m, KROW + face_index[m, f]] = 1.0
    slots = sends // wave_size
    regions = devices // wave_size
    rows = 4 * slots + 8 * (1 - fits(block, slots, width))
    faces = 4 * elements
    state = (9, NODES, elements)

    (message,) = call(
        functools.partial(gather_kernel, face_index),
        "hhhhh",
        (("w", (wave_size, rows, 128), F32),),
        scratch=(
            pltpu.VMEM((3, *state), F32),
            pltpu.VMEM((1, sends), jnp.int32),
            pltpu.VMEM((block, width), F32),
            pltpu.SemaphoreType.DMA((5,)),
        ),
        bytes_accessed=2 << 20,
        flops=1 << 28,
    )(state0, delta, adjoint, send_face.reshape(1, sends), coarse_step)
    got = lax.all_to_all(message, "wave", split_axis=0, concat_axis=0, tiled=True)
    own, vol0, vol1, vol2, lift_left, prolong_left, restrict_left, index, place, kind, places, speeds, half, normal = call(
        functools.partial(own_kernel, turning, regions, width),
        "w" * 16,
        (
            ("v", (ROWS, faces), F32),
            ("v", state, F32),
            ("x", state, F32),
            ("x", state, F32),
            ("v", (VROW, 192), BF16),
            ("v", (VROW, 240), BF16),
            ("v", (80, 3 * KROW), BF16),
            ("v", (16, faces), jnp.int32),
            ("v", (devices * width, elements), BF16),
            ("v", (8, elements), F32),
            ("v", (devices * deep, 4 * elements), BF16),
            ("v", (3, NODES, elements), F32),
            ("v", (4, elements), F32),
            ("v", (3, 4, elements), F32),
        ),
        scratch=(
            pltpu.VMEM((3 * VROW, 3 * KROW), F32),
            pltpu.VMEM((128, 128), F32),
            pltpu.VMEM((ROWS, faces), F32),
            pltpu.VMEM((ROWS, faces), BF16),
            pltpu.VMEM((ROWS, faces), BF16),
        ),
        limit=32 << 20,
        bytes_accessed=8 << 20,
        flops=1 << 32,
    )(
        state0,
        delta,
        adjoint,
        model,
        geometry,
        neighbor,
        orient,
        derivative,
        lift.transpose(2, 0, 1),
        prolong.transpose(2, 0, 1),
        jnp.asarray(np.pad(select, ((0, 0), (0, KROW))), BF16),
        normals,
        face_scale,
        owner.reshape(1, elements),
        coarse_local.reshape(1, elements),
        child.reshape(1, elements),
    )
    share = wave_size * width
    (near,) = call(
        functools.partial(pick_kernel, slots), "v", (("v", (32, share), F32),), limit=4 << 20
    )(got)
    blocks = [near] + [None] * (regions - 1)
    for s in reversed(range(1, regions)):
        blocks[s] = lax.ppermute(near, "region", [(i, i ^ s) for i in range(regions)])
    (jump,) = call(
        functools.partial(turn_kernel, slots),
        "vvvv",
        (("v", (ROWS, faces), F32),),
        bytes_accessed=2 << 20,
        flops=1 << 29,
    )(got, index, neighbor, own)
    base, moved, backed = call(
        flux_kernel, "vvvvvv", (("v", state, F32),) * 3, bytes_accessed=4 << 20, flops=1 << 30
    )(jump, lift_left, normal, half, vol0, speeds)
    moved, backed, seen = call(
        ready_kernel,
        "v" * 5,
        (("v", state, F32), ("v", state, F32), ("v", (NODES, elements), F32)),
        bytes_accessed=1 << 20,
        flops=1 << 22,
    )(moved, backed, observe, vol1, vol2)
    delta_next, adjoint_next, message = call(
        functools.partial(step_kernel, regions),
        "v" * (regions + 10),
        (("v", state, F32), ("v", state, F32), ("v", (devices, deep, 128), F32)),
        scratch=(pltpu.VMEM((2, 128, 4 * elements), BF16),),
        limit=12 << 20,
        bytes_accessed=4 << 20,
        flops=1 << 30,
    )(*blocks, base, moved, backed, prolong_left, restrict_left, place, kind, places, coarse_local.reshape(1, elements), seen)
    arrived = lax.all_to_all(message, everyone, split_axis=0, concat_axis=0, tiled=True)
    hess_vec, delta_next, adjoint_next = call(
        sum_kernel,
        "vvvvv",
        (("h", (block, width), F32), ("h", state, F32), ("h", state, F32)),
        scratch=(pltpu.VMEM((block, width), F32), pltpu.SemaphoreType.DMA((3,))),
        limit=4 << 20,
    )(arrived, reg_weight, coarse_step, delta_next, adjoint_next)
    return (delta_next, adjoint_next, hess_vec)


def solution(mesh):
    both = ("region", "wave")
    wide, flat = P(None, None, both), P(None, both)
    placed = (
        wide,
        wide,
        wide,
        wide,
        flat,
        wide,
        flat,
        P(),
        P(),
        P(),
        flat,
        flat,
        flat,
        P(both, None),
        P(both),
        P(both),
        flat,
        flat,
        P(both),
    )
    return jax.shard_map(
        body, mesh=mesh, in_specs=placed, out_specs=(wide, wide, flat), check_vma=False
    )
```
